512 devices in a mesh: gx: 8 (over y_lo, x), gy: 4 (over y_hi), gz: 16 (over z, core).
Axes of the slice: x: 4, y: 8 (y_hi: 4, y_lo: 2; y = y_hi * 2 + y_lo), z: 8, core: 2. Of those that a mesh axis runs over, the one named last changes fastest.
Arguments:
- source_term: float32 [64, 64, 2048], P('gx', 'gy', 'gz'), may hold values from -6 to 6
- conductivity: float32 [64, 64, 2048], P('gx', 'gy', 'gz'), may hold values from 0.3 to 3
- initial_guess: float32 [64, 64, 2048], P('gx', 'gy', 'gz'), may hold values from -4 to 4
- box_owner: int32 [8, 4, 16], replicated, may hold values from 0 to 3
Outputs:
- potential: float32 [64, 64, 2048], P('gx', 'gy', 'gz')
The draws below stay inside these ranges and needn't reach their ends.
Inputs may be any that keep to these rules, and one draw needn't show every extreme that they name: `box_owner`: labels of the coarse boxes; boxes with equal labels couple only within one plane of boxes along z.
All inputs are finite; a program needn't handle non-finite values.
Results may differ from the reference program's by a relative error of at most 0.0001.
Values sent between devices are 32-bit elements; how exact they have to be, the bound alone decides.
A program may use at most 64 MiB of HBM per device.

```python
import math
import jax
import jax.numpy as jnp

CX = 8
CY = 16
CZ = 128
CSWEEPS = 8
LABELS = 4
NX = 64
NY = 64
NZ = 2048
BX = 8
BY = 4
BZ = 16


def plant(entries, own_key, least, top_value):
    spot = [jax.random.randint(jax.random.fold_in(own_key, axis), (), 0, length) for axis, length in enumerate(entries.shape)]
    widest = entries.shape.index(max(entries.shape))
    neighbour = spot[:widest] + [(spot[widest] + 1) % entries.shape[widest]] + spot[widest + 1:]
    return entries.at[tuple(spot)].set(least).at[tuple(neighbour)].set(top_value)


def levels(stream_key, shape, split, least, high):
    factor_of, own = 1.0, jax.random.fold_in(stream_key, 6)
    for axis_at, parts in split:
        steps = jnp.exp(jax.random.uniform(jax.random.fold_in(own, axis_at), (parts,), jnp.float32, least / len(split), high / len(split)))
        factor_of = factor_of * jnp.repeat(steps, shape[axis_at] // parts).reshape([-1 if axis == axis_at else 1 for axis in range(len(shape))])
    return factor_of


def scatter_about(stream_key, shape, deviation, limit, shards=(), held_as=jnp.bfloat16):
    result = jax.random.normal(stream_key, shape, jnp.float32) * deviation
    if len(shards) > 0:
        result = levels(stream_key, shape, shards, -0.22, 0.18) * result
    return jnp.clip(result, min=-limit, max=limit).astype(held_as)


def setup_inputs(seed: int = 0) -> dict:
    keys = jax.random.split(jax.random.key(seed), 5)
    return {
        "source_term": scatter_about(keys[0], (NX, NY, NZ), 1.0, 6.0, ((0, 8), (1, 4), (2, 16)), jnp.float32),
        "conductivity": jnp.clip(jnp.exp(math.log(3.0) - 2.3025851 * jax.random.uniform(keys[1], (NX, NY, NZ), jnp.float32) ** levels(keys[1], (NX, NY, NZ), ((0, 8), (1, 4), (2, 16)), -0.2, 0.2)), 0.3, 3.0),
        "initial_guess": scatter_about(keys[2], (NX, NY, NZ), 0.5, 4.0, ((0, 8), (1, 4), (2, 16)), jnp.float32),
        "box_owner": plant(jax.random.randint(keys[3], (BX, BY, BZ), 0, LABELS), jax.random.fold_in(keys[3], 1), 0, LABELS - 1).astype(jnp.int32),
    }


screening = 0.05
offsets = ((-1, 0), (1, 0), (-1, 1), (1, 1), (-1, 2), (1, 2))


def coarsen(values):
    extent = values.shape
    return values.reshape(extent[0] // 2, 2, extent[1] // 2, 2, extent[2] // 2, 2).mean(axis=(1, 3, 5))


def refine(values):
    return jnp.repeat(jnp.repeat(jnp.repeat(values, 2, 0), 2, 1), 2, 2)


def face_weight(coef, index):
    return (coef + jnp.roll(coef, offsets[index][0], offsets[index][1])) * 0.5


def diagonal_of(coef, stiffness):
    total = face_weight(coef, 0)
    for index in range(1, 6):
        total = total + face_weight(coef, index)
    return screening + stiffness * total


def beside_all(field, coef, masks):
    total = None
    for index in range(6):
        weight = face_weight(coef, index)
        if masks is not None:
            weight = weight * masks[index].astype(jnp.float32)
        term = weight * jnp.roll(field, offsets[index][0], offsets[index][1])
        total = term if total is None else total + term
    return total


def parity_of(extent, z_offset):
    x_index = jnp.arange(extent[0], dtype=jnp.int32)
    y_index = jnp.arange(extent[1], dtype=jnp.int32)
    z_index = jnp.arange(extent[2], dtype=jnp.int32) + z_offset
    return (x_index[:, None, None] + y_index[None, :, None] + z_index[None, None, :]) % 2


def sweep_field(field, source, coef, masks, diagonal, stiffness):
    parity = parity_of(field.shape, 0)
    for colour in (0, 1):
        updated = (source + stiffness * beside_all(field, coef, masks)) / diagonal
        field = jnp.where(parity == colour, updated, field)
    return field


def reference(source_term, conductivity, initial_guess, box_owner):
    coefs = [conductivity]
    for _ in range(3):
        coefs.append(coarsen(coefs[-1]))
    field = initial_guess
    source = source_term
    saved = []
    for coarse_step in range(3):
        stiffness = 0.25 ** coarse_step
        coef = coefs[coarse_step]
        diagonal = diagonal_of(coef, stiffness)
        if coarse_step > 0:
            field = jnp.zeros(source.shape, jnp.float32)
        field = sweep_field(field, source, coef, None, diagonal, stiffness)
        residual = source - (diagonal * field - stiffness * beside_all(field, coef, None))
        saved.append((field, source))
        source = coarsen(residual)
    stiffness = 0.25 ** 3
    diagonal = diagonal_of(coefs[3], stiffness)
    labels = jnp.repeat(jnp.repeat(jnp.repeat(box_owner, CX // 8, 0), CY // 8, 1), CZ // 8, 2)
    extent = source.shape
    box_depth = CZ // 8
    z_local = jnp.arange(extent[2], dtype=jnp.int32) % box_depth
    z_up = jnp.broadcast_to((z_local != box_depth - 1)[None, None, :], extent)
    z_down = jnp.broadcast_to((z_local != 0)[None, None, :], extent)
    masks = (labels == jnp.roll(labels, -1, 0), labels == jnp.roll(labels, 1, 0),
             labels == jnp.roll(labels, -1, 1), labels == jnp.roll(labels, 1, 1), z_up, z_down)
    correction = jnp.zeros(extent, jnp.float32)
    for _ in range(CSWEEPS):
        correction = sweep_field(correction, source, coefs[3], masks, diagonal, stiffness)
    for coarse_step in (2, 1, 0):
        field, source = saved[coarse_step]
        stiffness = 0.25 ** coarse_step
        coef = coefs[coarse_step]
        diagonal = diagonal_of(coef, stiffness)
        field = sweep_field(field + refine(correction), source, coef, None, diagonal, stiffness)
        correction = field
    return correction
```

```python
import itertools

import jax
import jax.numpy as jnp
from jax import lax
from jax.experimental import pallas as pl
from jax.experimental.pallas import tpu as pltpu
from jax.sharding import PartitionSpec as P

MESH = pl.DeviceIdType.MESH
SX, SY, SZ = 8, 4, 16
CSWEEPS = 8
screening = 0.05

NEAR = [d for d in itertools.product((-1, 0, 1), repeat=3) if d != (0, 0, 0)]
CLOSE = [d for d in NEAR if abs(d[0]) + abs(d[1]) + abs(d[2]) <= 2]
PLANE = [d for d in itertools.product(range(SX), range(SY)) if d != (0, 0)]
ALONG = [-2, -1, 1, 2]


def everyone():
    found = {(a % SX, b % SY, c % SZ) for a, b, c in NEAR}
    found |= {(a, b, 0) for a, b in PLANE}
    found |= {(0, 0, c % SZ) for c in ALONG}
    return sorted(found)


def roll(values, shift, axis):
    shift = shift % values.shape[axis]
    return values if shift == 0 else pltpu.roll(values, shift, axis)


def around(before, here, after, step):
    return (
        after,
        before,
        roll(here, -1, 0),
        roll(here, 1, 0),
        roll(here, -step, 1),
        roll(here, step, 1),
    )


def faces(before, here, after, step, stiffness):
    half = 0.5 * stiffness
    weights = [half * (here + other) for other in around(before, here, after, step)]
    diagonal = screening + (
        (weights[0] + weights[1]) + (weights[2] + weights[3]) + (weights[4] + weights[5])
    )
    return weights, diagonal


def relaxed(level, scaled, before, here, after, step):
    sides = around(before, here, after, step)
    terms = [scaled[n] * sides[n] for n in range(6)]
    return level + (((terms[0] + terms[1]) + (terms[2] + terms[3])) + (terms[4] + terms[5]))


def pair_sum(values):
    lane = lax.broadcasted_iota(jnp.int32, values.shape, len(values.shape) - 1)
    return values + jnp.where(lane % 2 == 0, roll(values, -1, 1), roll(values, 1, 1))


def kernel(
    f_in, c_in, v_in, owner, out,
    E0, PK0, PZ0, A0, D0, U0, PKV, PZV, R0,
    E1, PK1, PZ1, A1, D1, V1, X1, R1,
    T2, ZR, S2, W2, V2, A2, D2, R2, E3, A3, B3,
    in_sem, a_s, a_r, c1_s, c1_r, b1_s, b1_r, v0_s, v0_r, z_s, z_r, m_s, m_r,
):
    me = (lax.axis_index("gx"), lax.axis_index("gy"), lax.axis_index("gz"))

    def at(d):
        return tuple(
            lax.rem(me[i] + d[i] + size, size) for i, size in enumerate((SX, SY, SZ))
        )

    def send(src, dst, send_sem, recv_sem, d):
        copy = pltpu.make_async_remote_copy(
            src_ref=src, dst_ref=dst, send_sem=send_sem, recv_sem=recv_sem,
            device_id=at(d), device_id_type=MESH,
        )
        copy.start()
        return copy

    loads = [
        pltpu.make_async_copy(ref, E0.at[pl.ds(3, 8), n, pl.ds(0, 16), pl.ds(0, 128)], in_sem.at[n])
        for n, ref in enumerate((v_in, c_in, f_in))
    ]
    for copy in loads:
        copy.start()
    barrier = pltpu.get_barrier_semaphore()
    others = everyone()
    for d in others:
        pl.semaphore_signal(barrier, inc=1, device_id=at(d), device_id_type=MESH)
    for copy in loads:
        copy.wait()

    lane16 = lax.broadcasted_iota(jnp.int32, (16, 128), 1)
    packed = jnp.zeros((16, 128), jnp.float32)
    for i in range(8):
        for n in range(3):
            lo, count = (16 * i + 6 * n, 6) if n < 2 else (16 * i + 12, 4)
            moved = roll(E0[3 + i, n, 0:16, 0:128], lo - (125 if n < 2 else 126), 1)
            packed = jnp.where((lane16 >= lo) & (lane16 < lo + count), moved, packed)
    PK0[...] = packed

    def coarsen0(get, store):
        for i in range(4):
            R0[i] = pair_sum(get(2 * i) + get(2 * i + 1))
        for i in range(4):
            store(i, 0.125 * (R0[i, pl.ds(0, 8, stride=2), :] + R0[i, pl.ds(1, 8, stride=2), :]))

    lane8 = lax.broadcasted_iota(jnp.int32, (8, 128), 1)

    def pack1(kind):
        tile = jnp.zeros((8, 128), jnp.float32)
        for i in range(4):
            moved = roll(E1[4 + i, kind, 0:8, 0:128], 16 * i - 120, 1)
            tile = jnp.where((lane8 >= 16 * i) & (lane8 < 16 * i + 16), moved, tile)
        PK1[kind] = tile

    row_of = lax.broadcasted_iota(jnp.int32, (128, 128), 0)
    col_of = lax.broadcasted_iota(jnp.int32, (128, 128), 1)
    squeeze = jnp.where(row_of // 4 == (col_of + 16) % 32, 0.25, 0.0).astype(jnp.float32)

    def coarsen1(get, kind):
        both = jnp.concatenate([get(0) + get(1), get(2) + get(3)], axis=0)
        R1[...] = jnp.dot(
            both, squeeze, precision=lax.Precision.HIGHEST, preferred_element_type=jnp.float32
        )
        T2[kind] = 0.25 * (R1[pl.ds(0, 8, stride=2), :] + R1[pl.ds(1, 8, stride=2), :])

    def put_c1(i, value):
        E1[4 + i, 0, 0:8, 0:128] = value

    coarsen0(lambda i: E0[3 + i, 1, 0:16, 0:128], put_c1)
    pack1(0)
    coarsen1(lambda i: E1[4 + i, 0, 0:8, 0:128], 0)

    pl.semaphore_wait(barrier, len(others))

    x_from = {0: (3, 8), 1: (8, 3), -1: (3, 3)}
    x_to = {0: (3, 8), 1: (0, 3), -1: (11, 3)}
    y_from = {0: (0, 16), 1: (13, 3), -1: (0, 3)}
    y_to = {0: (0, 16), 1: (21, 3), -1: (16, 3)}
    lanes = pl.ds(0, 128)

    def side_of(oz):
        return 0 if oz == -1 else 1

    copies_a = []
    for k, (ox, oy, oz) in enumerate(NEAR):
        if oz == 0:
            src = E0.at[pl.ds(*x_from[ox]), :, pl.ds(*y_from[oy]), lanes]
            dst = E0.at[pl.ds(*x_to[ox]), :, pl.ds(*y_to[oy]), lanes]
        else:
            src = PK0.at[pl.ds(*y_from[oy])]
            dst = PZ0.at[side_of(oz), 1 - ox, pl.ds(*y_to[oy])]
        copies_a.append(send(src, dst, a_s.at[k], a_r.at[k], (ox, oy, oz)))

    def swap1(kind, send_sem, recv_sem):
        xd = {0: 4, 1: 0, -1: 8}
        ys = {0: (0, 8), 1: (4, 4), -1: (0, 4)}
        yd = {0: (0, 8), 1: (12, 4), -1: (8, 4)}
        copies = []
        for k, (ox, oy, oz) in enumerate(NEAR):
            if oz == 0:
                src = E1.at[pl.ds(4, 4), kind, pl.ds(*ys[oy]), lanes]
                dst = E1.at[pl.ds(xd[ox], 4), kind, pl.ds(*yd[oy]), lanes]
            else:
                src = PK1.at[kind, pl.ds(*ys[oy])]
                dst = PZ1.at[kind, side_of(oz), 1 - ox, pl.ds(*yd[oy])]
            copies.append(send(src, dst, send_sem.at[k], recv_sem.at[k], (ox, oy, oz)))
        return copies

    def stage_z(kind):
        return [
            send(T2.at[kind], ZR.at[kind, k], z_s.at[kind, k], z_r.at[kind, k], (0, 0, oz))
            for k, oz in enumerate(ALONG)
        ]

    def window(kind):
        ahead2, ahead1, behind1, behind2 = (ZR[kind, k] for k in range(4))
        tile = jnp.where(lane8 < 16, behind2, behind1)
        tile = jnp.where(lane8 < 48, tile, T2[kind])
        tile = jnp.where(lane8 < 80, tile, ahead1)
        tile = jnp.where(lane8 < 112, tile, ahead2)
        for i in range(2):
            S2[kind, i, 0:4] = tile[4 * i : 4 * i + 4]
            W2[kind, i, 0:4] = tile[4 * i : 4 * i + 4]

    def stage_xy(kind):
        copies = []
        for k, (ox, oy) in enumerate(PLANE):
            dx, dy = (SX - ox) % SX, (SY - oy) % SY
            src = S2.at[kind, :, pl.ds(0, 4)]
            dst = W2.at[kind, pl.ds(2 * dx, 2), pl.ds(4 * dy, 4)]
            copies.append(send(src, dst, m_s.at[kind, k], m_r.at[kind, k], (ox, oy, 0)))
        return copies

    copies_c1 = swap1(0, c1_s, c1_r)
    copies_cz = stage_z(0)

    sub8 = lax.broadcasted_iota(jnp.int32, (8, 128), 0)
    labels = []
    for x in range(SX):
        bx = lax.rem(me[0] + x, SX)
        tile = jnp.zeros((8, 128), jnp.int32)
        for y in range(SY):
            by = lax.rem(me[1] + y, SY)
            low, mid, high = (
                owner[bx, by, lax.rem(me[2] + dz + SZ, SZ)] for dz in (-1, 0, 1)
            )
            part = jnp.where(lane8 < 48, low, jnp.where(lane8 < 80, mid, high))
            tile = jnp.where(sub8 // 2 == y, part, tile)
        labels.append(tile)

    for copy in copies_a:
        copy.wait_recv()
    for copy in copies_a:
        copy.wait_send()

    lane24 = lax.broadcasted_iota(jnp.int32, (24, 128), 1)
    slot = lane24 % 16
    from_below = (slot < 3) | ((slot >= 6) & (slot < 9)) | ((slot >= 12) & (slot < 14))
    for dx in range(3):
        both = jnp.where(from_below, PZ0[1, dx], PZ0[0, dx])
        for p in {0: range(0, 3), 1: range(3, 11), 2: range(11, 14)}[dx]:
            i = {0: p + 5, 1: p - 3, 2: p - 11}[dx]
            for n in range(3):
                lo, base = (16 * i + 6 * n, 125) if n < 2 else (16 * i + 12, 126)
                E0[p, n, :, 128:256] = roll(both, base - lo, 1)

    shape0 = (24, 256)
    par0 = (lax.broadcasted_iota(jnp.int32, shape0, 0) + lax.broadcasted_iota(jnp.int32, shape0, 1)) % 2

    def setup0(p, carry):
        weights, diagonal = faces(E0[p - 1, 1], E0[p, 1], E0[p + 1, 1], 1, 1.0)
        inverse = 1.0 / diagonal
        for n in range(6):
            A0[p, n] = weights[n] * inverse
        A0[p, 6] = E0[p, 2] * inverse
        D0[p] = diagonal
        return carry

    lax.fori_loop(1, 13, setup0, 0)

    def point_v(p):
        scaled = [A0[p, n] for n in range(6)]
        here = E0[p, 0]
        update = relaxed(A0[p, 6], scaled, E0[p - 1, 0], here, E0[p + 1, 0], 1)
        return update, here

    def pass_v(q):
        def body(p, carry):
            update, here = point_v(p)
            E0[p, 0] = jnp.where(par0 == (p + 1 + q) % 2, update, here)
            return carry
        return body

    lax.fori_loop(1, 13, pass_v(0), 0)
    lax.fori_loop(2, 12, pass_v(1), 0)

    packed = jnp.zeros((16, 128), jnp.float32)
    for i in range(8):
        moved = roll(E0[3 + i, 0, 0:16, 0:128], 16 * i - 126, 1)
        packed = jnp.where((lane16 >= 16 * i) & (lane16 < 16 * i + 4), moved, packed)
    PKV[...] = packed

    def resid0(i):
        update, here = point_v(3 + i)
        return (D0[3 + i] * (update - here))[0:16, 0:128]

    for copy in copies_c1:
        copy.wait_recv()

    def unpack1(kind):
        lane_16 = lax.broadcasted_iota(jnp.int32, (16, 128), 1)
        for dx in range(3):
            both = jnp.where(lane_16 % 16 < 8, PZ1[kind, 1, dx], PZ1[kind, 0, dx])
            for i in range(4):
                E1[4 * dx + i, kind, :, 128:256] = roll(both, 120 - 16 * i, 1)

    unpack1(0)

    def setup1(p, carry):
        weights, diagonal = faces(E1[p - 1, 0], E1[p, 0], E1[p + 1, 0], 2, 0.25)
        inverse = 1.0 / diagonal
        for n in range(6):
            A1[p, n] = weights[n] * inverse
        A1[p, 6] = inverse
        D1[p] = diagonal
        return carry

    lax.fori_loop(1, 11, setup1, 0)

    def put_b1(i, value):
        E1[4 + i, 1, 0:8, 0:128] = value * A1[4 + i, 6, 0:8, 0:128]

    coarsen0(resid0, put_b1)
    pack1(1)
    for copy in copies_c1:
        copy.wait_send()
    copies_b1 = swap1(1, b1_s, b1_r)

    xs = {0: (3, 8), 1: (9, 2), -1: (3, 2)}
    xd = {0: (2, 8), 1: (0, 2), -1: (10, 2)}
    ys = {0: (0, 16), 1: (14, 2), -1: (0, 2)}
    yd = {0: (0, 16), 1: (22, 2), -1: (16, 2)}
    copies_v0 = []
    for k, (ox, oy, oz) in enumerate(CLOSE):
        if oz == 0:
            src = E0.at[pl.ds(*xs[ox]), 0, pl.ds(*ys[oy]), lanes]
            dst = U0.at[pl.ds(*xd[ox]), pl.ds(*yd[oy]), lanes]
        else:
            src = PKV.at[pl.ds(*ys[oy])]
            dst = PZV.at[side_of(oz), 1 - ox, pl.ds(*yd[oy])]
        copies_v0.append(send(src, dst, v0_s.at[k], v0_r.at[k], (ox, oy, oz)))
    for i in range(8):
        U0[2 + i, 0:16, 0:128] = E0[3 + i, 0, 0:16, 0:128]

    for copy in copies_cz:
        copy.wait_recv()
    window(0)
    copies_cm = stage_xy(0)

    for copy in copies_b1:
        copy.wait_recv()

    unpack1(1)
    shape1 = (16, 256)
    par1 = (
        lax.broadcasted_iota(jnp.int32, shape1, 0) + lax.broadcasted_iota(jnp.int32, shape1, 1) // 2
    ) % 2
    for p in range(12):
        V1[p] = jnp.where(par1 == p % 2, E1[p, 1], 0.0)

    def point1(p):
        scaled = [A1[p, n] for n in range(6)]
        here = V1[p]
        return relaxed(E1[p, 1], scaled, V1[p - 1], here, V1[p + 1], 2), here

    def pass1(q):
        def body(p, carry):
            update, here = point1(p)
            V1[p] = jnp.where(par1 == (p + q) % 2, update, here)
            return carry
        return body

    lax.fori_loop(1, 11, pass1(1), 0)

    def resid1(i):
        update, here = point1(4 + i)
        return (D1[4 + i] * (update - here))[0:8, 0:128]

    coarsen1(resid1, 1)
    copies_fz = stage_z(1)

    for copy in copies_cm:
        copy.wait_recv()

    def setup2(p, carry):
        here = W2[0, p]
        weights, diagonal = faces(
            W2[0, lax.rem(p + 15, 16)], here, W2[0, lax.rem(p + 1, 16)], 1, 0.0625
        )
        inverse = 1.0 / diagonal
        for n in range(6):
            A2[p, n] = weights[n] * inverse
        A2[p, 6] = inverse
        D2[p] = diagonal
        return carry

    def coarsen2(get, store):
        for i in range(8):
            R2[i] = pair_sum(get(2 * i) + get(2 * i + 1))
        for i in range(8):
            store(i, 0.125 * (R2[i, pl.ds(0, 8, stride=2), :] + R2[i, pl.ds(1, 8, stride=2), :]))

    def put_c3(i, value):
        E3[i] = value

    for copy in copies_fz:
        copy.wait_recv()
    window(1)
    copies_fm = stage_xy(1)

    lax.fori_loop(0, 16, setup2, 0)
    coarsen2(lambda i: W2[0, i], put_c3)
    z3 = ((lane8 + 16) % 32) // 2
    for x in range(8):
        weights, diagonal = faces(E3[(x + 7) % 8], E3[x], E3[(x + 1) % 8], 2, 0.015625)
        inverse = 1.0 / diagonal
        label = labels[x]
        joined = (
            label == labels[(x + 1) % 8],
            label == labels[(x + 7) % 8],
            label == roll(label, -1, 0),
            label == roll(label, 1, 0),
            z3 != 15,
            z3 != 0,
        )
        for n in range(6):
            A3[x, n] = jnp.where(joined[n], weights[n] * inverse, 0.0)
        B3[x] = inverse

    for copy in copies_fm:
        copy.wait_recv()

    shape2 = (16, 128)
    par2 = (
        lax.broadcasted_iota(jnp.int32, shape2, 0) + lax.broadcasted_iota(jnp.int32, shape2, 1)
    ) % 2
    for p in range(16):
        W2[1, p] = W2[1, p] * A2[p, 6]
        V2[p] = jnp.where(par2 == p % 2, W2[1, p], 0.0)

    def point2(p):
        scaled = [A2[p, n] for n in range(6)]
        here = V2[p]
        before, after = V2[lax.rem(p + 15, 16)], V2[lax.rem(p + 1, 16)]
        return relaxed(W2[1, p], scaled, before, here, after, 1), here

    def pass2(q, start):
        def body(t, carry):
            p = lax.rem(t + start, 16)
            update, here = point2(p)
            V2[p] = jnp.where(par2 == (p + q) % 2, update, here)
            return carry
        return body

    lax.fori_loop(0, 16, pass2(1, 0), 0)

    def resid2(p):
        update, here = point2(p)
        return D2[p] * (update - here)

    def put_b3(i, value):
        B3[i] = value * B3[i]

    coarsen2(resid2, put_b3)

    par3 = (sub8 + lane8 // 2 + me[0]) % 2
    for x in range(8):
        E3[x] = jnp.where(par3 == x % 2, B3[x], 0.0)

    def pass3(q):
        for x in range(8):
            scaled = [A3[x, n] for n in range(6)]
            here = E3[x]
            update = relaxed(B3[x], scaled, E3[(x + 7) % 8], here, E3[(x + 1) % 8], 2)
            E3[x] = jnp.where(par3 == (x + q) % 2, update, here)

    pass3(1)

    def sweep3(t, carry):
        pass3(0)
        pass3(1)
        return carry

    lax.fori_loop(0, CSWEEPS - 1, sweep3, 0)

    for p in range(16):
        R2[p // 2, pl.ds(0, 8, stride=2), :] = E3[p // 2]
        R2[p // 2, pl.ds(1, 8, stride=2), :] = E3[p // 2]
    for p in range(16):
        V2[p] = V2[p] + R2[p // 2]
    lax.fori_loop(0, 8, pass2(0, 13), 0)
    lax.fori_loop(0, 6, pass2(1, 14), 0)

    wide_row = lax.broadcasted_iota(jnp.int32, (128, 256), 0)
    wide_col = lax.broadcasted_iota(jnp.int32, (128, 256), 1)
    beyond = wide_col - 128
    origin = jnp.where(
        wide_col < 128,
        48 + wide_col // 4,
        jnp.where(beyond < 64, 80 + beyond // 4, 16 + beyond // 4),
    )
    stretch = jnp.where(wide_row == origin, 1.0, 0.0).astype(jnp.float32)
    pieces = []
    for x in range(-2, 4):
        plane = V2[x % 16]
        pieces.append(jnp.where(sub8 < 6, plane[0:8], plane[8:16]))
    spread = jnp.dot(
        jnp.concatenate(pieces, axis=0), stretch,
        precision=lax.Precision.HIGHEST, preferred_element_type=jnp.float32,
    )
    for x in range(6):
        part = spread[8 * x : 8 * x + 8]
        for half in range(2):
            piece = part[:, 128 * half : 128 * half + 128]
            X1[x, half, pl.ds(0, 8, stride=2), :] = piece
            X1[x, half, pl.ds(1, 8, stride=2), :] = piece
    for p in range(1, 11):
        x = p - 4
        add = jnp.concatenate([X1[x // 2 + 2, 0], X1[x // 2 + 2, 1]], axis=1)
        V1[p] = V1[p] + add
    lax.fori_loop(2, 10, pass1(0), 0)
    lax.fori_loop(3, 9, pass1(1), 0)

    for copy in copies_v0:
        copy.wait_recv()
    for dx in range(3):
        both = jnp.where(lane24 % 16 < 2, PZV[1, dx], PZV[0, dx])
        for p in {0: range(0, 2), 1: range(2, 10), 2: range(10, 12)}[dx]:
            i = {0: p + 6, 1: p - 2, 2: p - 10}[dx]
            U0[p, :, 128:256] = roll(both, 126 - 16 * i, 1)
    sub256 = lax.broadcasted_iota(jnp.int32, (8, 256), 0)
    for j in range(6):
        value = V1[3 + j]
        for half in range(2):
            piece = value[0:8, 128 * half : 128 * half + 128]
            R0[half, pl.ds(0, 8, stride=2), :] = piece
            R0[half, pl.ds(1, 8, stride=2), :] = piece
        inner = jnp.concatenate([R0[0], R0[1]], axis=1)
        outer = jnp.where(
            sub256 < 4,
            jnp.broadcast_to(value[8:9], (8, 256)),
            jnp.broadcast_to(value[15:16], (8, 256)),
        )
        add = jnp.concatenate([inner, outer], axis=0)
        U0[2 * j] = U0[2 * j] + add
        U0[2 * j + 1] = U0[2 * j + 1] + add

    def point_u(p):
        scaled = [A0[p + 1, n] for n in range(6)]
        here = U0[p]
        return relaxed(A0[p + 1, 6], scaled, U0[p - 1], here, U0[p + 1], 1), here

    def up0(p, carry):
        update, here = point_u(p)
        U0[p] = jnp.where(par0 == p % 2, update, here)
        return carry

    lax.fori_loop(1, 11, up0, 0)

    def last0(p, carry):
        update, here = point_u(p)
        out[p - 2] = jnp.where(par0 == (p + 1) % 2, update, here)[0:16, 0:128]
        return carry

    lax.fori_loop(2, 10, last0, 0)

    for copies in (copies_cz, copies_b1, copies_v0, copies_cm, copies_fz, copies_fm):
        for copy in copies:
            copy.wait_send()


def local(source_term, conductivity, initial_guess, box_owner):
    def vmem(*shape):
        return pltpu.VMEM(shape, jnp.float32)

    dma = pltpu.SemaphoreType.DMA
    scratch = [
        vmem(14, 3, 24, 256), vmem(16, 128), vmem(2, 3, 24, 128), vmem(14, 7, 24, 256),
        vmem(14, 24, 256), vmem(12, 24, 256), vmem(16, 128), vmem(2, 3, 24, 128), vmem(4, 16, 128),
        vmem(12, 2, 16, 256), vmem(2, 8, 128), vmem(2, 2, 3, 16, 128), vmem(12, 7, 16, 256),
        vmem(12, 16, 256), vmem(12, 16, 256), vmem(6, 2, 16, 128), vmem(16, 128),
        vmem(2, 8, 128), vmem(2, 4, 8, 128), vmem(2, 2, 8, 128), vmem(2, 16, 16, 128),
        vmem(16, 16, 128), vmem(16, 7, 16, 128), vmem(16, 16, 128), vmem(8, 16, 128),
        vmem(8, 8, 128), vmem(8, 6, 8, 128), vmem(8, 8, 128),
        dma((3,)), dma((26,)), dma((26,)), dma((26,)), dma((26,)), dma((26,)), dma((26,)),
        dma((18,)), dma((18,)), dma((2, 4)), dma((2, 4)), dma((2, 31)), dma((2, 31)),
    ]
    anywhere = pl.BlockSpec(memory_space=pl.ANY)
    return pl.pallas_call(
        kernel,
        out_shape=jax.ShapeDtypeStruct(source_term.shape, jnp.float32),
        in_specs=[anywhere, anywhere, anywhere, pl.BlockSpec(memory_space=pltpu.SMEM)],
        out_specs=pl.BlockSpec(memory_space=pltpu.VMEM),
        scratch_shapes=scratch,
        compiler_params=pltpu.CompilerParams(
            collective_id=0, has_side_effects=True, vmem_limit_bytes=40 << 20
        ),
    )(source_term, conductivity, initial_guess, box_owner)


def solution(mesh):
    return jax.shard_map(
        local,
        mesh=mesh,
        in_specs=(P("gx", "gy", "gz"), P("gx", "gy", "gz"), P("gx", "gy", "gz"), P()),
        out_specs=P("gx", "gy", "gz"),
        check_vma=False,
    )
```

```python
import itertools

import jax
import jax.numpy as jnp
from jax import lax
from jax.experimental import pallas as pl
from jax.experimental.pallas import tpu as pltpu
from jax.sharding import PartitionSpec as P

MESH = pl.DeviceIdType.MESH
SX, SY, SZ = 8, 4, 16
CSWEEPS = 8
screening = 0.05

NEAR = [d for d in itertools.product((-1, 0, 1), repeat=3) if d != (0, 0, 0)]
CLOSE = [d for d in NEAR if abs(d[0]) + abs(d[1]) + abs(d[2]) <= 2]
PLANE = [d for d in itertools.product(range(SX), range(SY)) if d != (0, 0)]
ALONG = [-2, -1, 1, 2]


def everyone():
    found = {(a % SX, b % SY, c % SZ) for a, b, c in NEAR}
    found |= {(a, b, 0) for a, b in PLANE}
    found |= {(0, 0, c % SZ) for c in ALONG}
    return sorted(found)


def roll(values, shift, axis):
    shift = shift % values.shape[axis]
    return values if shift == 0 else pltpu.roll(values, shift, axis)


def around(before, here, after, step):
    return (
        after,
        before,
        roll(here, -1, 0),
        roll(here, 1, 0),
        roll(here, -step, 1),
        roll(here, step, 1),
    )


def faces(before, here, after, step, stiffness):
    half = 0.5 * stiffness
    weights = [half * (here + other) for other in around(before, here, after, step)]
    diagonal = screening + (
        (weights[0] + weights[1]) + (weights[2] + weights[3]) + (weights[4] + weights[5])
    )
    return weights, diagonal


def relaxed(level, scaled, before, here, after, step):
    sides = around(before, here, after, step)
    terms = [scaled[n] * sides[n] for n in range(6)]
    return level + (((terms[0] + terms[1]) + (terms[2] + terms[3])) + (terms[4] + terms[5]))


def beyond_block(x, count):
    return max(0, -x, x - count + 1)


def quarters(away, reach, rows, all_rows):
    inner = (slice(0, rows), slice(0, 128))
    found = [inner]
    if away + 1 <= reach:
        found += [(slice(rows, all_rows), slice(0, 128)), (slice(0, rows), slice(128, 256))]
    if away + 2 <= reach:
        found.append((slice(rows, all_rows), slice(128, 256)))
    return found


def pair_sum(values):
    lane = lax.broadcasted_iota(jnp.int32, values.shape, len(values.shape) - 1)
    return values + jnp.where(lane % 2 == 0, roll(values, -1, 1), roll(values, 1, 1))


def kernel(
    f_in, c_in, v_in, owner_in, out,
    E0, PK0, PZ0, A0, D0, VA, VB, U0, UA, UB, PKV, PZV, R0, X0,
    E1, PK1, PZ1, A1, D1, V1, V1B, V1C, V1D, X1, R1,
    T2, ZR, S2, W2, V2, V2B, V2C, A2, D2, R2, E3, A3, B3, owner,
    in_sem, a_s, a_r, c1_s, c1_r, b1_s, b1_r, v0_s, v0_r, z_s, z_r, m_s, m_r,
):
    me = (lax.axis_index("gx"), lax.axis_index("gy"), lax.axis_index("gz"))

    def at(d):
        return tuple(
            lax.rem(me[i] + d[i] + size, size) for i, size in enumerate((SX, SY, SZ))
        )

    def send(src, dst, send_sem, recv_sem, d):
        copy = pltpu.make_async_remote_copy(
            src_ref=src, dst_ref=dst, send_sem=send_sem, recv_sem=recv_sem,
            device_id=at(d), device_id_type=MESH,
        )
        copy.start()
        return copy

    loads = [
        pltpu.make_async_copy(ref, E0.at[pl.ds(3, 8), n, pl.ds(0, 16), pl.ds(0, 128)], in_sem.at[n])
        for n, ref in enumerate((v_in, c_in, f_in))
    ]
    loads.append(pltpu.make_async_copy(owner_in, owner, in_sem.at[3]))
    for copy in loads:
        copy.start()
    barrier = pltpu.get_barrier_semaphore()
    others = everyone()
    for d in others:
        pl.semaphore_signal(barrier, inc=1, device_id=at(d), device_id_type=MESH)
    for copy in loads:
        copy.wait()

    lane16 = lax.broadcasted_iota(jnp.int32, (16, 128), 1)
    packed = jnp.zeros((16, 128), jnp.float32)
    for i in range(8):
        for n in range(3):
            lo, count = (16 * i + 6 * n, 6) if n < 2 else (16 * i + 12, 4)
            moved = roll(E0[3 + i, n, 0:16, 0:128], lo - (125 if n < 2 else 126), 1)
            packed = jnp.where((lane16 >= lo) & (lane16 < lo + count), moved, packed)
    PK0[...] = packed

    def coarsen0(get, store):
        for i in range(4):
            R0[i] = pair_sum(get(2 * i) + get(2 * i + 1))
        for i in range(4):
            store(i, 0.125 * (R0[i, pl.ds(0, 8, stride=2), :] + R0[i, pl.ds(1, 8, stride=2), :]))

    lane8 = lax.broadcasted_iota(jnp.int32, (8, 128), 1)

    def pack1(kind):
        tile = jnp.zeros((8, 128), jnp.float32)
        for i in range(4):
            moved = roll(E1[4 + i, kind, 0:8, 0:128], 16 * i - 120, 1)
            tile = jnp.where((lane8 >= 16 * i) & (lane8 < 16 * i + 16), moved, tile)
        PK1[kind] = tile

    row_of = lax.broadcasted_iota(jnp.int32, (128, 128), 0)
    col_of = lax.broadcasted_iota(jnp.int32, (128, 128), 1)
    squeeze = jnp.where(row_of // 4 == (col_of + 16) % 32, 0.25, 0.0).astype(jnp.float32)

    def coarsen1(get, kind):
        both = jnp.concatenate([get(0) + get(1), get(2) + get(3)], axis=0)
        R1[...] = jnp.dot(
            both, squeeze, precision=lax.Precision.HIGHEST, preferred_element_type=jnp.float32
        )
        T2[kind] = 0.25 * (R1[pl.ds(0, 8, stride=2), :] + R1[pl.ds(1, 8, stride=2), :])

    def put_c1(i, value):
        E1[4 + i, 0, 0:8, 0:128] = value

    coarsen0(lambda i: E0[3 + i, 1, 0:16, 0:128], put_c1)
    pack1(0)
    coarsen1(lambda i: E1[4 + i, 0, 0:8, 0:128], 0)

    pl.semaphore_wait(barrier, len(others))

    x_from = {0: (3, 8), 1: (8, 3), -1: (3, 3)}
    x_to = {0: (3, 8), 1: (0, 3), -1: (11, 3)}
    y_from = {0: (0, 16), 1: (13, 3), -1: (0, 3)}
    y_to = {0: (0, 16), 1: (21, 3), -1: (16, 3)}
    lanes = pl.ds(0, 128)

    def side_of(oz):
        return 0 if oz == -1 else 1

    copies_a = []
    for k, (ox, oy, oz) in enumerate(NEAR):
        if oz == 0:
            src = E0.at[pl.ds(*x_from[ox]), :, pl.ds(*y_from[oy]), lanes]
            dst = E0.at[pl.ds(*x_to[ox]), :, pl.ds(*y_to[oy]), lanes]
        else:
            src = PK0.at[pl.ds(*y_from[oy])]
            dst = PZ0.at[side_of(oz), 1 - ox, pl.ds(*y_to[oy])]
        copies_a.append(send(src, dst, a_s.at[k], a_r.at[k], (ox, oy, oz)))

    def swap1(kind, send_sem, recv_sem):
        xd = {0: 4, 1: 0, -1: 8}
        ys = {0: (0, 8), 1: (4, 4), -1: (0, 4)}
        yd = {0: (0, 8), 1: (12, 4), -1: (8, 4)}
        copies = []
        for k, (ox, oy, oz) in enumerate(NEAR):
            if oz == 0:
                src = E1.at[pl.ds(4, 4), kind, pl.ds(*ys[oy]), lanes]
                dst = E1.at[pl.ds(xd[ox], 4), kind, pl.ds(*yd[oy]), lanes]
            else:
                src = PK1.at[kind, pl.ds(*ys[oy])]
                dst = PZ1.at[kind, side_of(oz), 1 - ox, pl.ds(*yd[oy])]
            copies.append(send(src, dst, send_sem.at[k], recv_sem.at[k], (ox, oy, oz)))
        return copies

    def stage_z(kind):
        return [
            send(T2.at[kind], ZR.at[kind, k], z_s.at[kind, k], z_r.at[kind, k], (0, 0, oz))
            for k, oz in enumerate(ALONG)
        ]

    def window(kind):
        ahead2, ahead1, behind1, behind2 = (ZR[kind, k] for k in range(4))
        tile = jnp.where(lane8 < 16, behind2, behind1)
        tile = jnp.where(lane8 < 48, tile, T2[kind])
        tile = jnp.where(lane8 < 80, tile, ahead1)
        tile = jnp.where(lane8 < 112, tile, ahead2)
        for i in range(2):
            S2[kind, i, 0:4] = tile[4 * i : 4 * i + 4]
            W2[kind, i, 0:4] = tile[4 * i : 4 * i + 4]

    def stage_xy(kind):
        copies = []
        for k, (ox, oy) in enumerate(PLANE):
            dx, dy = (SX - ox) % SX, (SY - oy) % SY
            src = S2.at[kind, :, pl.ds(0, 4)]
            dst = W2.at[kind, pl.ds(2 * dx, 2), pl.ds(4 * dy, 4)]
            copies.append(send(src, dst, m_s.at[kind, k], m_r.at[kind, k], (ox, oy, 0)))
        return copies

    copies_c1 = swap1(0, c1_s, c1_r)
    copies_cz = stage_z(0)

    sub8 = lax.broadcasted_iota(jnp.int32, (8, 128), 0)
    labels = []
    for x in range(SX):
        bx = lax.rem(me[0] + x, SX)
        tile = jnp.zeros((8, 128), jnp.int32)
        for y in range(SY):
            by = lax.rem(me[1] + y, SY)
            low, mid, high = (
                owner[bx, by, lax.rem(me[2] + dz + SZ, SZ)] for dz in (-1, 0, 1)
            )
            part = jnp.where(lane8 < 48, low, jnp.where(lane8 < 80, mid, high))
            tile = jnp.where(sub8 // 2 == y, part, tile)
        labels.append(tile)

    for copy in copies_a:
        copy.wait_recv()

    lane24 = lax.broadcasted_iota(jnp.int32, (24, 128), 1)
    slot = lane24 % 16
    from_below = (slot < 3) | ((slot >= 6) & (slot < 9)) | ((slot >= 12) & (slot < 14))
    for dx in range(3):
        both = jnp.where(from_below, PZ0[1, dx], PZ0[0, dx])
        for p in {0: range(0, 3), 1: range(3, 11), 2: range(11, 14)}[dx]:
            i = {0: p + 5, 1: p - 3, 2: p - 11}[dx]
            for n in range(3):
                lo, base = (16 * i + 6 * n, 125) if n < 2 else (16 * i + 12, 126)
                E0[p, n, :, 128:256] = roll(both, base - lo, 1)

    shape0 = (24, 256)
    par0 = (lax.broadcasted_iota(jnp.int32, shape0, 0) + lax.broadcasted_iota(jnp.int32, shape0, 1)) % 2

    for p in range(1, 13):
        weights, diagonal = faces(E0[p - 1, 1], E0[p, 1], E0[p + 1, 1], 1, 1.0)
        inverse = 1.0 / diagonal
        level = E0[p, 2] * inverse
        for rows, cols in quarters(beyond_block(p - 3, 8), 2, 16, 24):
            for n in range(6):
                A0[p, n, rows, cols] = (weights[n] * inverse)[rows, cols]
            A0[p, 6, rows, cols] = level[rows, cols]
        if 3 <= p < 11:
            D0[p - 3] = diagonal[0:16, 0:128]

    def point0(get, p):
        scaled = [A0[p, n] for n in range(6)]
        here = get(p)
        return relaxed(A0[p, 6], scaled, get(p - 1), here, get(p + 1), 1), here

    def colour0(get, store, planes, q, reach):
        for p in planes:
            update, here = point0(get, p)
            mixed = jnp.where(par0 == (p + 1 + q) % 2, update, here)
            for rows, cols in quarters(beyond_block(p - 3, 8), reach, 16, 24):
                store(p, rows, cols, mixed[rows, cols])

    def get_e(p):
        return E0[p, 0]

    def get_va(p):
        return VA[p - 1]

    def put_va(p, rows, cols, value):
        VA[p - 1, rows, cols] = value

    def get_vb(p):
        return VB[p - 2]

    def put_vb(p, rows, cols, value):
        VB[p - 2, rows, cols] = value

    colour0(get_e, put_va, range(1, 13), 0, 2)
    colour0(get_va, put_vb, range(2, 12), 1, 1)

    def resid0(i):
        update, here = point0(get_vb, 3 + i)
        return D0[i] * (update - here)[0:16, 0:128]

    for copy in copies_c1:
        copy.wait_recv()

    def unpack1(kind):
        lane_16 = lax.broadcasted_iota(jnp.int32, (16, 128), 1)
        for dx in range(3):
            both = jnp.where(lane_16 % 16 < 8, PZ1[kind, 1, dx], PZ1[kind, 0, dx])
            for i in range(4):
                E1[4 * dx + i, kind, :, 128:256] = roll(both, 120 - 16 * i, 1)

    unpack1(0)

    def setup1(p):
        weights, diagonal = faces(E1[p - 1, 0], E1[p, 0], E1[p + 1, 0], 2, 0.25)
        inverse = 1.0 / diagonal
        for n in range(6):
            A1[p, n] = weights[n] * inverse
        if 4 <= p < 8:
            D1[p - 4] = diagonal[0:8, 0:128]

    own1 = []
    for p in range(4, 8):
        own1.append(1.0 / faces(E1[p - 1, 0], E1[p, 0], E1[p + 1, 0], 2, 0.25)[1][0:8, 0:128])

    def put_b1(i, value):
        E1[4 + i, 1, 0:8, 0:128] = value * own1[i]

    coarsen0(resid0, put_b1)
    pack1(1)
    copies_b1 = swap1(1, b1_s, b1_r)

    packed = jnp.zeros((16, 128), jnp.float32)
    for i in range(8):
        moved = roll(VB[1 + i, 0:16, 0:128], 16 * i - 126, 1)
        packed = jnp.where((lane16 >= 16 * i) & (lane16 < 16 * i + 4), moved, packed)
    PKV[...] = packed
    xs = {0: (1, 8), 1: (7, 2), -1: (1, 2)}
    xd = {0: (2, 8), 1: (0, 2), -1: (10, 2)}
    ys = {0: (0, 16), 1: (14, 2), -1: (0, 2)}
    yd = {0: (0, 16), 1: (22, 2), -1: (16, 2)}
    copies_v0 = []
    for k, (ox, oy, oz) in enumerate(CLOSE):
        if oz == 0:
            src = VB.at[pl.ds(*xs[ox]), pl.ds(*ys[oy]), lanes]
            dst = U0.at[pl.ds(*xd[ox]), pl.ds(*yd[oy]), lanes]
        else:
            src = PKV.at[pl.ds(*ys[oy])]
            dst = PZV.at[side_of(oz), 1 - ox, pl.ds(*yd[oy])]
        copies_v0.append(send(src, dst, v0_s.at[k], v0_r.at[k], (ox, oy, oz)))
    for i in range(8):
        U0[2 + i, 0:16, 0:128] = VB[1 + i, 0:16, 0:128]

    for p in range(1, 11):
        setup1(p)

    for copy in copies_cz:
        copy.wait_recv()
    window(0)
    copies_cm = stage_xy(0)

    for copy in copies_b1:
        copy.wait_recv()

    unpack1(1)
    shape1 = (16, 256)
    par1 = (
        lax.broadcasted_iota(jnp.int32, shape1, 0) + lax.broadcasted_iota(jnp.int32, shape1, 1) // 2
    ) % 2
    first1 = [jnp.where(par1 == p % 2, E1[p, 1], 0.0) for p in range(12)]

    def point1(get, p):
        scaled = [A1[p, n] for n in range(6)]
        here = get(p)
        return relaxed(E1[p, 1], scaled, get(p - 1), here, get(p + 1), 2), here

    def colour1(get, store, planes, q, reach):
        for p in planes:
            update, here = point1(get, p)
            mixed = jnp.where(par1 == (p + q) % 2, update, here)
            for rows, cols in quarters(beyond_block(p - 4, 4), reach, 8, 16):
                store(p, rows, cols, mixed[rows, cols])

    def getter(ref):
        return lambda p: ref[p]

    def putter(ref):
        def put(p, rows, cols, value):
            ref[p, rows, cols] = value
        return put

    colour1(lambda p: first1[p], putter(V1), range(1, 11), 1, 4)

    def resid1(i):
        update, here = point1(getter(V1), 4 + i)
        return D1[i] * (update - here)[0:8, 0:128]

    coarsen1(resid1, 1)
    copies_fz = stage_z(1)

    for copy in copies_cm:
        copy.wait_recv()

    def setup2(p):
        here = W2[0, p]
        weights, diagonal = faces(W2[0, (p + 15) % 16], here, W2[0, (p + 1) % 16], 1, 0.0625)
        inverse = 1.0 / diagonal
        for n in range(6):
            A2[p, n] = weights[n] * inverse
        A2[p, 6] = inverse
        D2[p] = diagonal

    def coarsen2(get, store):
        for i in range(8):
            R2[i] = pair_sum(get(2 * i) + get(2 * i + 1))
        for i in range(8):
            store(i, 0.125 * (R2[i, pl.ds(0, 8, stride=2), :] + R2[i, pl.ds(1, 8, stride=2), :]))

    def put_c3(i, value):
        E3[i] = value

    for copy in copies_fz:
        copy.wait_recv()
    window(1)
    copies_fm = stage_xy(1)

    for p in range(16):
        setup2(p)
    coarsen2(lambda i: W2[0, i], put_c3)
    z3 = ((lane8 + 16) % 32) // 2
    for x in range(8):
        weights, diagonal = faces(E3[(x + 7) % 8], E3[x], E3[(x + 1) % 8], 2, 0.015625)
        inverse = 1.0 / diagonal
        label = labels[x]
        joined = (
            label == labels[(x + 1) % 8],
            label == labels[(x + 7) % 8],
            label == roll(label, -1, 0),
            label == roll(label, 1, 0),
            z3 != 15,
            z3 != 0,
        )
        for n in range(6):
            A3[x, n] = jnp.where(joined[n], weights[n] * inverse, 0.0)
        B3[x] = inverse

    for copy in copies_fm:
        copy.wait_recv()

    shape2 = (16, 128)
    par2 = (
        lax.broadcasted_iota(jnp.int32, shape2, 0) + lax.broadcasted_iota(jnp.int32, shape2, 1)
    ) % 2
    level2 = [W2[1, p] * A2[p, 6] for p in range(16)]
    first2 = [jnp.where(par2 == p % 2, level2[p], 0.0) for p in range(16)]
    for p in range(16):
        W2[1, p] = level2[p]

    def point2(get, p):
        scaled = [A2[p, n] for n in range(6)]
        here = get(p)
        return relaxed(W2[1, p], scaled, get((p + 15) % 16), here, get((p + 1) % 16), 1), here

    def colour2(get, ref, planes, q):
        for t in planes:
            p = t % 16
            update, here = point2(get, p)
            ref[p] = jnp.where(par2 == (p + q) % 2, update, here)

    colour2(lambda p: first2[p], V2, range(16), 1)

    def resid2(p):
        update, here = point2(getter(V2), p)
        return D2[p] * (update - here)

    def put_b3(i, value):
        B3[i] = value * B3[i]

    coarsen2(resid2, put_b3)

    par3 = (sub8 + lane8 // 2 + me[0]) % 2
    def pass3(values, q):
        fresh = []
        for x in range(8):
            scaled = [A3[x, n] for n in range(6)]
            here = values[x]
            update = relaxed(B3[x], scaled, values[(x + 7) % 8], here, values[(x + 1) % 8], 2)
            fresh.append(jnp.where(par3 == (x + q) % 2, update, here))
        return tuple(fresh)

    solved = tuple(jnp.where(par3 == x % 2, B3[x], 0.0) for x in range(8))
    solved = pass3(solved, 1)
    solved = lax.fori_loop(
        0, CSWEEPS - 1, lambda t, values: pass3(pass3(values, 0), 1), solved
    )

    for x in (6, 7, 0, 1, 2):
        R2[x, pl.ds(0, 8, stride=2), :] = solved[x]
        R2[x, pl.ds(1, 8, stride=2), :] = solved[x]
    for t in range(12, 22):
        p = t % 16
        V2B[p] = V2[p] + R2[p // 2]
    colour2(getter(V2B), V2C, range(13, 21), 0)
    colour2(getter(V2C), V2B, range(14, 20), 1)

    wide_row = lax.broadcasted_iota(jnp.int32, (128, 256), 0)
    wide_col = lax.broadcasted_iota(jnp.int32, (128, 256), 1)
    beyond = wide_col - 128
    origin = jnp.where(
        wide_col < 128,
        48 + wide_col // 4,
        jnp.where(beyond < 64, 80 + beyond // 4, 16 + beyond // 4),
    )
    stretch = jnp.where(wide_row == origin, 1.0, 0.0).astype(jnp.float32)
    pieces = []
    for x in range(-2, 4):
        plane = V2B[x % 16]
        pieces.append(jnp.where(sub8 < 6, plane[0:8], plane[8:16]))
    spread = jnp.dot(
        jnp.concatenate(pieces, axis=0), stretch,
        precision=lax.Precision.HIGHEST, preferred_element_type=jnp.float32,
    )
    for x in range(6):
        part = spread[8 * x : 8 * x + 8]
        for half in range(2):
            piece = part[:, 128 * half : 128 * half + 128]
            X1[x, half, pl.ds(0, 8, stride=2), :] = piece
            X1[x, half, pl.ds(1, 8, stride=2), :] = piece
    for p in range(1, 11):
        x = p - 4
        add = jnp.concatenate([X1[x // 2 + 2, 0], X1[x // 2 + 2, 1]], axis=1)
        V1B[p] = V1[p] + add
    colour1(getter(V1B), putter(V1C), range(2, 10), 0, 3)
    colour1(getter(V1C), putter(V1D), range(3, 9), 1, 2)

    for copy in copies_v0:
        copy.wait_recv()
    for dx in range(3):
        both = jnp.where(lane24 % 16 < 2, PZV[1, dx], PZV[0, dx])
        for p in {0: range(0, 2), 1: range(2, 10), 2: range(10, 12)}[dx]:
            i = {0: p + 6, 1: p - 2, 2: p - 10}[dx]
            U0[p, :, 128:256] = roll(both, 126 - 16 * i, 1)
    sub256 = lax.broadcasted_iota(jnp.int32, (8, 256), 0)
    for j in range(6):
        value = V1D[3 + j]
        for half in range(2):
            piece = value[0:8, 128 * half : 128 * half + 128]
            X0[j, half, pl.ds(0, 8, stride=2), :] = piece
            X0[j, half, pl.ds(1, 8, stride=2), :] = piece
        inner = jnp.concatenate([X0[j, 0], X0[j, 1]], axis=1)
        outer = jnp.where(
            sub256 < 4,
            jnp.broadcast_to(value[8:9], (8, 256)),
            jnp.broadcast_to(value[15:16], (8, 256)),
        )
        add = jnp.concatenate([inner, outer], axis=0)
        UA[2 * j] = U0[2 * j] + add
        UA[2 * j + 1] = U0[2 * j + 1] + add

    def get_ua(p):
        return UA[p - 1]

    def get_ub(p):
        return UB[p - 2]

    def put_ub(p, rows, cols, value):
        UB[p - 2, rows, cols] = value

    def put_out(p, rows, cols, value):
        out[p - 3] = value

    colour0(get_ua, put_ub, range(2, 12), 0, 1)
    colour0(get_ub, put_out, range(3, 11), 1, 0)

    for copies in (copies_a, copies_c1, copies_cz, copies_b1, copies_v0, copies_cm, copies_fz, copies_fm):
        for copy in copies:
            copy.wait_send()


def local(source_term, conductivity, initial_guess, box_owner):
    def vmem(*shape):
        return pltpu.VMEM(shape, jnp.float32)

    dma = pltpu.SemaphoreType.DMA
    scratch = [
        vmem(14, 3, 24, 256), vmem(16, 128), vmem(2, 3, 24, 128), vmem(14, 7, 24, 256),
        vmem(8, 16, 128), vmem(12, 24, 256), vmem(10, 24, 256), vmem(12, 24, 256),
        vmem(12, 24, 256), vmem(10, 24, 256), vmem(16, 128), vmem(2, 3, 24, 128),
        vmem(4, 16, 128), vmem(6, 2, 16, 128),
        vmem(12, 2, 16, 256), vmem(2, 8, 128), vmem(2, 2, 3, 16, 128), vmem(12, 6, 16, 256),
        vmem(4, 8, 128), vmem(12, 16, 256), vmem(12, 16, 256), vmem(12, 16, 256),
        vmem(12, 16, 256), vmem(6, 2, 16, 128), vmem(16, 128),
        vmem(2, 8, 128), vmem(2, 4, 8, 128), vmem(2, 2, 8, 128), vmem(2, 16, 16, 128),
        vmem(16, 16, 128), vmem(16, 16, 128), vmem(16, 16, 128), vmem(16, 7, 16, 128),
        vmem(16, 16, 128), vmem(8, 16, 128), vmem(8, 8, 128), vmem(8, 6, 8, 128),
        vmem(8, 8, 128),
        pltpu.SMEM((8, 4, 16), jnp.int32),
        dma((4,)), dma((26,)), dma((26,)), dma((26,)), dma((26,)), dma((26,)), dma((26,)),
        dma((18,)), dma((18,)), dma((2, 4)), dma((2, 4)), dma((2, 31)), dma((2, 31)),
    ]
    anywhere = pl.BlockSpec(memory_space=pltpu.HBM)
    return pl.pallas_call(
        kernel,
        out_shape=jax.ShapeDtypeStruct(source_term.shape, jnp.float32),
        in_specs=[anywhere, anywhere, anywhere, anywhere],
        out_specs=pl.BlockSpec(memory_space=pltpu.VMEM),
        scratch_shapes=scratch,
        compiler_params=pltpu.CompilerParams(
            collective_id=0, has_side_effects=True, vmem_limit_bytes=60 << 20
        ),
    )(source_term, conductivity, initial_guess, box_owner)


def solution(mesh):
    return jax.shard_map(
        local,
        mesh=mesh,
        in_specs=(P("gx", "gy", "gz"), P("gx", "gy", "gz"), P("gx", "gy", "gz"), P()),
        out_specs=P("gx", "gy", "gz"),
        check_vma=False,
    )
```

```python
import itertools

import jax
import jax.numpy as jnp
from jax import lax
from jax.experimental import pallas as pl
from jax.experimental.pallas import tpu as pltpu
from jax.sharding import PartitionSpec as P

MESH = pl.DeviceIdType.MESH
SX, SY, SZ = 8, 4, 16
CSWEEPS = 8
screening = 0.05

NEAR = [d for d in itertools.product((-1, 0, 1), repeat=3) if d != (0, 0, 0)]
CLOSE = [d for d in NEAR if abs(d[0]) + abs(d[1]) + abs(d[2]) <= 2]
PLANE = [d for d in itertools.product(range(SX), range(SY)) if d != (0, 0)]
ALONG = [-2, -1, 1, 2]


def everyone():
    found = {(a % SX, b % SY, c % SZ) for a, b, c in NEAR}
    found |= {(a, b, 0) for a, b in PLANE}
    found |= {(0, 0, c % SZ) for c in ALONG}
    return sorted(found)


def roll(values, shift, axis):
    shift = shift % values.shape[axis]
    return values if shift == 0 else pltpu.roll(values, shift, axis)


def around(before, here, after, step):
    return (
        after,
        before,
        roll(here, -1, 0),
        roll(here, 1, 0),
        roll(here, -step, 1),
        roll(here, step, 1),
    )


def faces(before, here, after, step, stiffness):
    half = 0.5 * stiffness
    weights = [half * (here + other) for other in around(before, here, after, step)]
    diagonal = screening + (
        (weights[0] + weights[1]) + (weights[2] + weights[3]) + (weights[4] + weights[5])
    )
    return weights, diagonal


def relaxed(level, scaled, before, here, after, step):
    sides = around(before, here, after, step)
    terms = [scaled[n] * sides[n] for n in range(6)]
    return level + (((terms[0] + terms[1]) + (terms[2] + terms[3])) + (terms[4] + terms[5]))


def beyond_block(x, count):
    return max(0, -x, x - count + 1)


def quarters(away, reach, rows, all_rows):
    inner = (slice(0, rows), slice(0, 128))
    found = [inner]
    if away + 1 <= reach:
        found += [(slice(rows, all_rows), slice(0, 128)), (slice(0, rows), slice(128, 256))]
    if away + 2 <= reach:
        found.append((slice(rows, all_rows), slice(128, 256)))
    return found


def pair_sum(values):
    lane = lax.broadcasted_iota(jnp.int32, values.shape, len(values.shape) - 1)
    return values + jnp.where(lane % 2 == 0, roll(values, -1, 1), roll(values, 1, 1))


def kernel(
    f_in, c_in, v_in, owner_in, out,
    E0, PK0, PZ0, A0, D0, VA, VB, U0, UA, UB, PKV, PZV, R0, X0,
    C1, E1, PK1, PZ1, A1, D1, V1, V1B, V1C, V1D, X1, R1,
    T2, ZR, S2, W2, V2, V2B, V2C, A2, D2, R2, E3, A3, B3, owner,
    in_sem, a_s, a_r, c1_s, c1_r, b1_s, b1_r, v0_s, v0_r, z_s, z_r, m_s, m_r,
):
    me = (lax.axis_index("gx"), lax.axis_index("gy"), lax.axis_index("gz"))

    def at(d):
        return tuple(
            lax.rem(me[i] + d[i] + size, size) for i, size in enumerate((SX, SY, SZ))
        )

    def send(src, dst, send_sem, recv_sem, d):
        copy = pltpu.make_async_remote_copy(
            src_ref=src, dst_ref=dst, send_sem=send_sem, recv_sem=recv_sem,
            device_id=at(d), device_id_type=MESH,
        )
        copy.start()
        return copy

    loads = [
        pltpu.make_async_copy(ref, E0.at[pl.ds(3, 8), n, pl.ds(0, 16), pl.ds(0, 128)], in_sem.at[n])
        for n, ref in enumerate((v_in, c_in, f_in))
    ]
    loads.append(pltpu.make_async_copy(owner_in, owner, in_sem.at[3]))
    for copy in loads:
        copy.start()
    barrier = pltpu.get_barrier_semaphore()
    others = everyone()
    for d in others:
        pl.semaphore_signal(barrier, inc=1, device_id=at(d), device_id_type=MESH)
    for copy in loads:
        copy.wait()

    lane16 = lax.broadcasted_iota(jnp.int32, (16, 128), 1)
    packed = jnp.zeros((16, 128), jnp.float32)
    for i in range(8):
        for n in range(3):
            lo, count = (16 * i + 6 * n, 6) if n < 2 else (16 * i + 12, 4)
            moved = roll(E0[3 + i, n, 0:16, 0:128], lo - (125 if n < 2 else 126), 1)
            packed = jnp.where((lane16 >= lo) & (lane16 < lo + count), moved, packed)
    PK0[...] = packed

    def coarsen0(get, store):
        for i in range(4):
            R0[i] = pair_sum(get(2 * i) + get(2 * i + 1))
        for i in range(4):
            store(i, 0.125 * (R0[i, pl.ds(0, 8, stride=2), :] + R0[i, pl.ds(1, 8, stride=2), :]))

    lane8 = lax.broadcasted_iota(jnp.int32, (8, 128), 1)

    def pack1(kind):
        tile = jnp.zeros((8, 128), jnp.float32)
        for i in range(4):
            moved = roll(E1[4 + i, kind, 0:8, 0:128], 16 * i - 120, 1)
            tile = jnp.where((lane8 >= 16 * i) & (lane8 < 16 * i + 16), moved, tile)
        PK1[kind] = tile

    row_of = lax.broadcasted_iota(jnp.int32, (128, 128), 0)
    col_of = lax.broadcasted_iota(jnp.int32, (128, 128), 1)
    squeeze = jnp.where(row_of // 4 == (col_of + 16) % 32, 0.25, 0.0).astype(jnp.float32)

    def coarsen1(get, kind):
        both = jnp.concatenate([get(0) + get(1), get(2) + get(3)], axis=0)
        R1[...] = jnp.dot(
            both, squeeze, precision=lax.Precision.HIGHEST, preferred_element_type=jnp.float32
        )
        T2[kind] = 0.25 * (R1[pl.ds(0, 8, stride=2), :] + R1[pl.ds(1, 8, stride=2), :])

    def put_c1(i, value):
        E1[4 + i, 0, 0:8, 0:128] = value

    coarsen0(lambda i: E0[3 + i, 1, 0:16, 0:128], put_c1)
    pack1(0)
    coarsen1(lambda i: E1[4 + i, 0, 0:8, 0:128], 0)

    pl.semaphore_wait(barrier, len(others))

    def side_of(oz):
        return 0 if oz == -1 else 1

    def reach0(offset, width, count, low, high):
        if offset == 0:
            return (low, count), (low, count)
        if offset == 1:
            return (low + count - width, width), (high - width, width)
        return (low, width), (low + count, width)

    lanes = pl.ds(0, 128)

    copies_a = []
    for k, (ox, oy, oz) in enumerate(NEAR):
        width = 4 - abs(ox) - abs(oy) - abs(oz)
        (ys, yc), (yd, _) = reach0(oy, width, 16, 0, 24)
        if oz == 0:
            (xs, xc), _ = reach0(ox, width, 8, 3, 3)
            xd = {0: 3, 1: 3 - width, -1: 11}[ox]
            parts = [(0, 3, xs, xc, xd, ys, yc, yd)]
            if width == 3:
                (ys2, yc2), (yd2, _) = reach0(oy, 2, 16, 0, 24)
                (xs2, xc2), _ = reach0(ox, 2, 8, 3, 3)
                xd2 = {0: 3, 1: 1, -1: 11}[ox]
                parts = [(0, 2, xs, xc, xd, ys, yc, yd), (2, 1, xs2, xc2, xd2, ys2, yc2, yd2)]
            for j, (n, count, xs, xc, xd, ys, yc, yd) in enumerate(parts):
                src = E0.at[pl.ds(xs, xc), pl.ds(n, count), pl.ds(ys, yc), lanes]
                dst = E0.at[pl.ds(xd, xc), pl.ds(n, count), pl.ds(yd, yc), lanes]
                copies_a.append(send(src, dst, a_s.at[k, j], a_r.at[k, j], (ox, oy, oz)))
        else:
            src = PK0.at[pl.ds(ys, yc)]
            dst = PZ0.at[side_of(oz), 1 - ox, pl.ds(yd, yc)]
            copies_a.append(send(src, dst, a_s.at[k, 0], a_r.at[k, 0], (ox, oy, oz)))

    def swap1(kind, send_sem, recv_sem):
        xd = {0: 4, 1: 0, -1: 8}
        ys = {0: (0, 8), 1: (4, 4), -1: (0, 4)}
        yd = {0: (0, 8), 1: (12, 4), -1: (8, 4)}
        copies = []
        for k, (ox, oy, oz) in enumerate(NEAR):
            if oz == 0:
                src = E1.at[pl.ds(4, 4), kind, pl.ds(*ys[oy]), lanes]
                dst = E1.at[pl.ds(xd[ox], 4), kind, pl.ds(*yd[oy]), lanes]
            else:
                src = PK1.at[kind, pl.ds(*ys[oy])]
                dst = PZ1.at[kind, side_of(oz), 1 - ox, pl.ds(*yd[oy])]
            copies.append(send(src, dst, send_sem.at[k], recv_sem.at[k], (ox, oy, oz)))
        return copies

    def stage_z(kind):
        return [
            send(T2.at[kind], ZR.at[kind, k], z_s.at[kind, k], z_r.at[kind, k], (0, 0, oz))
            for k, oz in enumerate(ALONG)
        ]

    def window(kind):
        ahead2, ahead1, behind1, behind2 = (ZR[kind, k] for k in range(4))
        tile = jnp.where(lane8 < 16, behind2, behind1)
        tile = jnp.where(lane8 < 48, tile, T2[kind])
        tile = jnp.where(lane8 < 80, tile, ahead1)
        tile = jnp.where(lane8 < 112, tile, ahead2)
        for i in range(2):
            S2[kind, i, 0:4] = tile[4 * i : 4 * i + 4]
            W2[kind, i, 0:4] = tile[4 * i : 4 * i + 4]

    def stage_xy(kind):
        copies = []
        for k, (ox, oy) in enumerate(PLANE):
            dx, dy = (SX - ox) % SX, (SY - oy) % SY
            src = S2.at[kind, :, pl.ds(0, 4)]
            dst = W2.at[kind, pl.ds(2 * dx, 2), pl.ds(4 * dy, 4)]
            copies.append(send(src, dst, m_s.at[kind, k], m_r.at[kind, k], (ox, oy, 0)))
        return copies

    copies_cz = stage_z(0)
    copies_c1 = swap1(0, c1_s, c1_r)

    sub8 = lax.broadcasted_iota(jnp.int32, (8, 128), 0)
    labels = []
    for x in range(SX):
        bx = lax.rem(me[0] + x, SX)
        tile = jnp.zeros((8, 128), jnp.int32)
        for y in range(SY):
            by = lax.rem(me[1] + y, SY)
            low, mid, high = (
                owner[bx, by, lax.rem(me[2] + dz + SZ, SZ)] for dz in (-1, 0, 1)
            )
            part = jnp.where(lane8 < 48, low, jnp.where(lane8 < 80, mid, high))
            tile = jnp.where(sub8 // 2 == y, part, tile)
        labels.append(tile)

    for copy in copies_a:
        copy.wait_recv()

    lane24 = lax.broadcasted_iota(jnp.int32, (24, 128), 1)
    slot = lane24 % 16
    from_below = (slot < 3) | ((slot >= 6) & (slot < 9)) | ((slot >= 12) & (slot < 14))
    for dx in range(3):
        both = jnp.where(from_below, PZ0[1, dx], PZ0[0, dx])
        for p in {0: range(0, 3), 1: range(3, 11), 2: range(11, 14)}[dx]:
            i = {0: p + 5, 1: p - 3, 2: p - 11}[dx]
            for n in range(3):
                lo, base = (16 * i + 6 * n, 125) if n < 2 else (16 * i + 12, 126)
                E0[p, n, :, 128:256] = roll(both, base - lo, 1)

    shape0 = (24, 256)
    par0 = (lax.broadcasted_iota(jnp.int32, shape0, 0) + lax.broadcasted_iota(jnp.int32, shape0, 1)) % 2

    for p in range(1, 13):
        weights, diagonal = faces(E0[p - 1, 1], E0[p, 1], E0[p + 1, 1], 1, 1.0)
        inverse = 1.0 / diagonal
        level = E0[p, 2] * inverse
        for rows, cols in quarters(beyond_block(p - 3, 8), 2, 16, 24):
            for n in range(6):
                A0[p, n, rows, cols] = (weights[n] * inverse)[rows, cols]
            A0[p, 6, rows, cols] = level[rows, cols]
        if 3 <= p < 11:
            D0[p - 3] = diagonal[0:16, 0:128]

    def point0(get, p):
        scaled = [A0[p, n] for n in range(6)]
        here = get(p)
        return relaxed(A0[p, 6], scaled, get(p - 1), here, get(p + 1), 1), here

    def colour0(get, store, planes, q, reach):
        for p in planes:
            update, here = point0(get, p)
            mixed = jnp.where(par0 == (p + 1 + q) % 2, update, here)
            for rows, cols in quarters(beyond_block(p - 3, 8), reach, 16, 24):
                store(p, rows, cols, mixed[rows, cols])

    def get_e(p):
        return E0[p, 0]

    def get_va(p):
        return VA[p - 1]

    def put_va(p, rows, cols, value):
        VA[p - 1, rows, cols] = value

    def get_vb(p):
        return VB[p - 2]

    def put_vb(p, rows, cols, value):
        VB[p - 2, rows, cols] = value

    colour0(get_e, put_va, range(1, 13), 0, 2)
    colour0(get_va, put_vb, range(2, 12), 1, 1)

    def resid0(i):
        update, here = point0(get_vb, 3 + i)
        return D0[i] * (update - here)[0:16, 0:128]

    def unpack1(kind):
        lane_16 = lax.broadcasted_iota(jnp.int32, (16, 128), 1)
        for dx in range(3):
            both = jnp.where(lane_16 % 16 < 8, PZ1[kind, 1, dx], PZ1[kind, 0, dx])
            for i in range(4):
                E1[4 * dx + i, kind, :, 128:256] = roll(both, 120 - 16 * i, 1)

    def setup1(p):
        weights, diagonal = faces(E1[p - 1, 0], E1[p, 0], E1[p + 1, 0], 2, 0.25)
        inverse = 1.0 / diagonal
        for n in range(6):
            A1[p, n] = weights[n] * inverse
        if 4 <= p < 8:
            D1[p - 4] = diagonal[0:8, 0:128]

    near1 = []
    sub256 = lax.broadcasted_iota(jnp.int32, (8, 256), 0)
    for i in range(6):
        both = pair_sum(E0[2 * i + 1, 1] + E0[2 * i + 2, 1])
        for half in range(2):
            C1[i, half] = both[:, 128 * half : 128 * half + 128]
        rows = []
        for first, count in ((0, 8), (16, 1), (22, 1)):
            if count == 8:
                halves = [C1[i, h, pl.ds(0, 8, stride=2), :] + C1[i, h, pl.ds(1, 8, stride=2), :] for h in range(2)]
                rows.append(jnp.concatenate(halves, axis=1))
            else:
                rows.append(jnp.broadcast_to(both[first : first + 1] + both[first + 1 : first + 2], (8, 256)))
        near1.append(
            0.125 * jnp.concatenate([rows[0], jnp.where(sub256 < 4, rows[1], rows[2])], axis=0)
        )
    own1 = []
    for i in range(4):
        diagonal = faces(near1[i], near1[i + 1], near1[i + 2], 2, 0.25)[1]
        own1.append(1.0 / diagonal[0:8, 0:128])

    def put_b1(i, value):
        E1[4 + i, 1, 0:8, 0:128] = value * own1[i]

    coarsen0(resid0, put_b1)
    pack1(1)
    copies_b1 = swap1(1, b1_s, b1_r)

    packed = jnp.zeros((16, 128), jnp.float32)
    for i in range(8):
        moved = roll(VB[1 + i, 0:16, 0:128], 16 * i - 126, 1)
        packed = jnp.where((lane16 >= 16 * i) & (lane16 < 16 * i + 4), moved, packed)
    PKV[...] = packed
    xs = {0: (1, 8), 1: (7, 2), -1: (1, 2)}
    xd = {0: (2, 8), 1: (0, 2), -1: (10, 2)}
    ys = {0: (0, 16), 1: (14, 2), -1: (0, 2)}
    yd = {0: (0, 16), 1: (22, 2), -1: (16, 2)}
    copies_v0 = []
    for k, (ox, oy, oz) in enumerate(CLOSE):
        if oz == 0:
            src = VB.at[pl.ds(*xs[ox]), pl.ds(*ys[oy]), lanes]
            dst = U0.at[pl.ds(*xd[ox]), pl.ds(*yd[oy]), lanes]
        else:
            src = PKV.at[pl.ds(*ys[oy])]
            dst = PZV.at[side_of(oz), 1 - ox, pl.ds(*yd[oy])]
        copies_v0.append(send(src, dst, v0_s.at[k], v0_r.at[k], (ox, oy, oz)))
    for i in range(8):
        U0[2 + i, 0:16, 0:128] = VB[1 + i, 0:16, 0:128]

    for copy in copies_c1:
        copy.wait_recv()
    unpack1(0)
    for p in range(1, 11):
        setup1(p)

    for copy in copies_cz:
        copy.wait_recv()
    window(0)
    copies_cm = stage_xy(0)

    for copy in copies_b1:
        copy.wait_recv()

    unpack1(1)
    shape1 = (16, 256)
    par1 = (
        lax.broadcasted_iota(jnp.int32, shape1, 0) + lax.broadcasted_iota(jnp.int32, shape1, 1) // 2
    ) % 2
    first1 = [jnp.where(par1 == p % 2, E1[p, 1], 0.0) for p in range(12)]

    def point1(get, p):
        scaled = [A1[p, n] for n in range(6)]
        here = get(p)
        return relaxed(E1[p, 1], scaled, get(p - 1), here, get(p + 1), 2), here

    def colour1(get, store, planes, q, reach):
        for p in planes:
            update, here = point1(get, p)
            mixed = jnp.where(par1 == (p + q) % 2, update, here)
            for rows, cols in quarters(beyond_block(p - 4, 4), reach, 8, 16):
                store(p, rows, cols, mixed[rows, cols])

    def getter(ref):
        return lambda p: ref[p]

    def putter(ref):
        def put(p, rows, cols, value):
            ref[p, rows, cols] = value
        return put

    colour1(lambda p: first1[p], putter(V1), range(1, 11), 1, 4)

    def resid1(i):
        update, here = point1(getter(V1), 4 + i)
        return D1[i] * (update - here)[0:8, 0:128]

    coarsen1(resid1, 1)
    copies_fz = stage_z(1)

    for copy in copies_cm:
        copy.wait_recv()

    def setup2(p):
        here = W2[0, p]
        weights, diagonal = faces(W2[0, (p + 15) % 16], here, W2[0, (p + 1) % 16], 1, 0.0625)
        inverse = 1.0 / diagonal
        for n in range(6):
            A2[p, n] = weights[n] * inverse
        A2[p, 6] = inverse
        D2[p] = diagonal

    def coarsen2(get, store):
        for i in range(8):
            R2[i] = pair_sum(get(2 * i) + get(2 * i + 1))
        for i in range(8):
            store(i, 0.125 * (R2[i, pl.ds(0, 8, stride=2), :] + R2[i, pl.ds(1, 8, stride=2), :]))

    def put_c3(i, value):
        E3[i] = value

    for copy in copies_fz:
        copy.wait_recv()
    window(1)
    copies_fm = stage_xy(1)

    for p in range(16):
        setup2(p)
    coarsen2(lambda i: W2[0, i], put_c3)
    z3 = ((lane8 + 16) % 32) // 2
    for x in range(8):
        weights, diagonal = faces(E3[(x + 7) % 8], E3[x], E3[(x + 1) % 8], 2, 0.015625)
        inverse = 1.0 / diagonal
        label = labels[x]
        joined = (
            label == labels[(x + 1) % 8],
            label == labels[(x + 7) % 8],
            label == roll(label, -1, 0),
            label == roll(label, 1, 0),
            z3 != 15,
            z3 != 0,
        )
        for n in range(6):
            A3[x, n] = jnp.where(joined[n], weights[n] * inverse, 0.0)
        B3[x] = inverse

    for copy in copies_fm:
        copy.wait_recv()

    shape2 = (16, 128)
    par2 = (
        lax.broadcasted_iota(jnp.int32, shape2, 0) + lax.broadcasted_iota(jnp.int32, shape2, 1)
    ) % 2
    level2 = [W2[1, p] * A2[p, 6] for p in range(16)]
    first2 = [jnp.where(par2 == p % 2, level2[p], 0.0) for p in range(16)]
    for p in range(16):
        W2[1, p] = level2[p]

    def point2(get, p):
        scaled = [A2[p, n] for n in range(6)]
        here = get(p)
        return relaxed(W2[1, p], scaled, get((p + 15) % 16), here, get((p + 1) % 16), 1), here

    def colour2(get, ref, planes, q):
        for t in planes:
            p = t % 16
            update, here = point2(get, p)
            ref[p] = jnp.where(par2 == (p + q) % 2, update, here)

    colour2(lambda p: first2[p], V2, range(16), 1)

    def resid2(p):
        update, here = point2(getter(V2), p)
        return D2[p] * (update - here)

    def put_b3(i, value):
        B3[i] = value * B3[i]

    coarsen2(resid2, put_b3)

    par3 = (sub8 + lane8 // 2 + me[0]) % 2
    def pass3(values, q):
        fresh = []
        for x in range(8):
            scaled = [A3[x, n] for n in range(6)]
            here = values[x]
            update = relaxed(B3[x], scaled, values[(x + 7) % 8], here, values[(x + 1) % 8], 2)
            fresh.append(jnp.where(par3 == (x + q) % 2, update, here))
        return tuple(fresh)

    solved = tuple(jnp.where(par3 == x % 2, B3[x], 0.0) for x in range(8))
    solved = pass3(solved, 1)
    solved = lax.fori_loop(
        0, CSWEEPS - 1, lambda t, values: pass3(pass3(values, 0), 1), solved
    )

    for x in (6, 7, 0, 1, 2):
        R2[x, pl.ds(0, 8, stride=2), :] = solved[x]
        R2[x, pl.ds(1, 8, stride=2), :] = solved[x]
    for t in range(12, 22):
        p = t % 16
        V2B[p] = V2[p] + R2[p // 2]
    colour2(getter(V2B), V2C, range(13, 21), 0)
    colour2(getter(V2C), V2B, range(14, 20), 1)

    wide_row = lax.broadcasted_iota(jnp.int32, (128, 256), 0)
    wide_col = lax.broadcasted_iota(jnp.int32, (128, 256), 1)
    beyond = wide_col - 128
    origin = jnp.where(
        wide_col < 128,
        48 + wide_col // 4,
        jnp.where(beyond < 64, 80 + beyond // 4, 16 + beyond // 4),
    )
    stretch = jnp.where(wide_row == origin, 1.0, 0.0).astype(jnp.float32)
    pieces = []
    for x in range(-2, 4):
        plane = V2B[x % 16]
        pieces.append(jnp.where(sub8 < 6, plane[0:8], plane[8:16]))
    spread = jnp.dot(
        jnp.concatenate(pieces, axis=0), stretch,
        precision=lax.Precision.HIGHEST, preferred_element_type=jnp.float32,
    )
    for x in range(6):
        part = spread[8 * x : 8 * x + 8]
        for half in range(2):
            piece = part[:, 128 * half : 128 * half + 128]
            X1[x, half, pl.ds(0, 8, stride=2), :] = piece
            X1[x, half, pl.ds(1, 8, stride=2), :] = piece
    for p in range(1, 11):
        x = p - 4
        add = jnp.concatenate([X1[x // 2 + 2, 0], X1[x // 2 + 2, 1]], axis=1)
        V1B[p] = V1[p] + add
    colour1(getter(V1B), putter(V1C), range(2, 10), 0, 3)
    colour1(getter(V1C), putter(V1D), range(3, 9), 1, 2)

    for copy in copies_v0:
        copy.wait_recv()
    for dx in range(3):
        both = jnp.where(lane24 % 16 < 2, PZV[1, dx], PZV[0, dx])
        for p in {0: range(0, 2), 1: range(2, 10), 2: range(10, 12)}[dx]:
            i = {0: p + 6, 1: p - 2, 2: p - 10}[dx]
            U0[p, :, 128:256] = roll(both, 126 - 16 * i, 1)
    for j in range(6):
        value = V1D[3 + j]
        for half in range(2):
            piece = value[0:8, 128 * half : 128 * half + 128]
            X0[j, half, pl.ds(0, 8, stride=2), :] = piece
            X0[j, half, pl.ds(1, 8, stride=2), :] = piece
        inner = jnp.concatenate([X0[j, 0], X0[j, 1]], axis=1)
        outer = jnp.where(
            sub256 < 4,
            jnp.broadcast_to(value[8:9], (8, 256)),
            jnp.broadcast_to(value[15:16], (8, 256)),
        )
        add = jnp.concatenate([inner, outer], axis=0)
        UA[2 * j] = U0[2 * j] + add
        UA[2 * j + 1] = U0[2 * j + 1] + add

    def get_ua(p):
        return UA[p - 1]

    def get_ub(p):
        return UB[p - 2]

    def put_ub(p, rows, cols, value):
        UB[p - 2, rows, cols] = value

    def put_out(p, rows, cols, value):
        out[p - 3] = value

    colour0(get_ua, put_ub, range(2, 12), 0, 1)
    colour0(get_ub, put_out, range(3, 11), 1, 0)

    for copies in (copies_a, copies_c1, copies_cz, copies_b1, copies_v0, copies_cm, copies_fz, copies_fm):
        for copy in copies:
            copy.wait_send()


def local(source_term, conductivity, initial_guess, box_owner):
    def vmem(*shape):
        return pltpu.VMEM(shape, jnp.float32)

    dma = pltpu.SemaphoreType.DMA
    scratch = [
        vmem(14, 3, 24, 256), vmem(16, 128), vmem(2, 3, 24, 128), vmem(14, 7, 24, 256),
        vmem(8, 16, 128), vmem(12, 24, 256), vmem(10, 24, 256), vmem(12, 24, 256),
        vmem(12, 24, 256), vmem(10, 24, 256), vmem(16, 128), vmem(2, 3, 24, 128),
        vmem(4, 16, 128), vmem(6, 2, 16, 128),
        vmem(6, 2, 24, 128), vmem(12, 2, 16, 256), vmem(2, 8, 128), vmem(2, 2, 3, 16, 128), vmem(12, 6, 16, 256),
        vmem(4, 8, 128), vmem(12, 16, 256), vmem(12, 16, 256), vmem(12, 16, 256),
        vmem(12, 16, 256), vmem(6, 2, 16, 128), vmem(16, 128),
        vmem(2, 8, 128), vmem(2, 4, 8, 128), vmem(2, 2, 8, 128), vmem(2, 16, 16, 128),
        vmem(16, 16, 128), vmem(16, 16, 128), vmem(16, 16, 128), vmem(16, 7, 16, 128),
        vmem(16, 16, 128), vmem(8, 16, 128), vmem(8, 8, 128), vmem(8, 6, 8, 128),
        vmem(8, 8, 128),
        pltpu.SMEM((8, 4, 16), jnp.int32),
        dma((4,)), dma((26, 2)), dma((26, 2)), dma((26,)), dma((26,)), dma((26,)), dma((26,)),
        dma((18,)), dma((18,)), dma((2, 4)), dma((2, 4)), dma((2, 31)), dma((2, 31)),
    ]
    anywhere = pl.BlockSpec(memory_space=pltpu.HBM)
    return pl.pallas_call(
        kernel,
        out_shape=jax.ShapeDtypeStruct(source_term.shape, jnp.float32),
        in_specs=[anywhere, anywhere, anywhere, anywhere],
        out_specs=pl.BlockSpec(memory_space=pltpu.VMEM),
        scratch_shapes=scratch,
        compiler_params=pltpu.CompilerParams(
            collective_id=0, has_side_effects=True, vmem_limit_bytes=55120 << 10
        ),
    )(source_term, conductivity, initial_guess, box_owner)


def solution(mesh):
    return jax.shard_map(
        local,
        mesh=mesh,
        in_specs=(P("gx", "gy", "gz"), P("gx", "gy", "gz"), P("gx", "gy", "gz"), P()),
        out_specs=P("gx", "gy", "gz"),
        check_vma=False,
    )
```

```python
import itertools

import jax
import jax.numpy as jnp
from jax import lax
from jax.experimental import pallas as pl
from jax.experimental.pallas import tpu as pltpu
from jax.sharding import PartitionSpec as P

MESH = pl.DeviceIdType.MESH
SX, SY, SZ = 8, 4, 16
CSWEEPS = 8
screening = 0.05

NEAR = [d for d in itertools.product((-1, 0, 1), repeat=3) if d != (0, 0, 0)]
NEAR.sort(key=lambda d: (-2 * abs(d[1]) - abs(d[0]) - abs(d[2]) / 2, d))
CLOSE = [d for d in NEAR if abs(d[0]) + abs(d[1]) + abs(d[2]) <= 2]
PLANE = [d for d in itertools.product(range(SX), range(SY)) if d != (0, 0)]
ALONG = [-2, -1, 1, 2]


def everyone():
    found = {(a % SX, b % SY, c % SZ) for a, b, c in NEAR}
    found |= {(a, b, 0) for a, b in PLANE}
    found |= {(0, 0, c % SZ) for c in ALONG}
    return sorted(found)


def roll(values, shift, axis):
    shift = shift % values.shape[axis]
    return values if shift == 0 else pltpu.roll(values, shift, axis)


def around(before, here, after, step):
    return (
        after,
        before,
        roll(here, -1, 0),
        roll(here, 1, 0),
        roll(here, -step, 1),
        roll(here, step, 1),
    )


def faces(before, here, after, step, stiffness):
    half = 0.5 * stiffness
    weights = [half * (here + other) for other in around(before, here, after, step)]
    diagonal = screening + (
        (weights[0] + weights[1]) + (weights[2] + weights[3]) + (weights[4] + weights[5])
    )
    return weights, diagonal


def relaxed(level, scaled, before, here, after, step):
    sides = around(before, here, after, step)
    terms = [scaled[n] * sides[n] for n in range(6)]
    return level + (((terms[0] + terms[1]) + (terms[2] + terms[3])) + (terms[4] + terms[5]))


def beyond_block(x, count):
    return max(0, -x, x - count + 1)


def quarters(away, reach, rows, all_rows):
    inner = (slice(0, rows), slice(0, 128))
    found = [inner]
    if away + 1 <= reach:
        found += [(slice(rows, all_rows), slice(0, 128)), (slice(0, rows), slice(128, 256))]
    if away + 2 <= reach:
        found.append((slice(rows, all_rows), slice(128, 256)))
    return found


def pair_sum(values):
    lane = lax.broadcasted_iota(jnp.int32, values.shape, len(values.shape) - 1)
    return values + jnp.where(lane % 2 == 0, roll(values, -1, 1), roll(values, 1, 1))


def kernel(
    f_in, c_in, v_in, owner_in, out,
    E0, PK0, PZ0, A0, D0, VA, VB, U0, UA, UB, PKV, PZV, R0, X0,
    C1, E1, PK1, PZ1, A1, D1, V1, V1B, V1C, V1D, X1, R1,
    T2, ZR, S2, W2, V2, V2B, V2C, A2, D2, R2, E3, A3, B3, owner,
    in_sem, a_s, a_r, c1_s, c1_r, b1_s, b1_r, v0_s, v0_r, z_s, z_r, m_s, m_r,
):
    me = (lax.axis_index("gx"), lax.axis_index("gy"), lax.axis_index("gz"))

    def at(d):
        return tuple(
            lax.rem(me[i] + d[i] + size, size) for i, size in enumerate((SX, SY, SZ))
        )

    def send(src, dst, send_sem, recv_sem, d):
        copy = pltpu.make_async_remote_copy(
            src_ref=src, dst_ref=dst, send_sem=send_sem, recv_sem=recv_sem,
            device_id=at(d), device_id_type=MESH,
        )
        copy.start()
        return copy

    loads = [
        pltpu.make_async_copy(ref, E0.at[pl.ds(3, 8), n, pl.ds(0, 16), pl.ds(0, 128)], in_sem.at[n])
        for n, ref in enumerate((v_in, c_in, f_in))
    ]
    loads.append(pltpu.make_async_copy(owner_in, owner, in_sem.at[3]))
    for copy in loads:
        copy.start()
    barrier = pltpu.get_barrier_semaphore()
    others = everyone()
    for d in others:
        pl.semaphore_signal(barrier, inc=1, device_id=at(d), device_id_type=MESH)
    for copy in loads:
        copy.wait()

    lane16 = lax.broadcasted_iota(jnp.int32, (16, 128), 1)
    packed = jnp.zeros((16, 128), jnp.float32)
    for i in range(8):
        for n in range(3):
            lo, count = (16 * i + 6 * n, 6) if n < 2 else (16 * i + 12, 4)
            moved = roll(E0[3 + i, n, 0:16, 0:128], lo - (125 if n < 2 else 126), 1)
            packed = jnp.where((lane16 >= lo) & (lane16 < lo + count), moved, packed)
    PK0[...] = packed

    def coarsen0(get, store):
        for i in range(4):
            R0[i] = pair_sum(get(2 * i) + get(2 * i + 1))
        for i in range(4):
            store(i, 0.125 * (R0[i, pl.ds(0, 8, stride=2), :] + R0[i, pl.ds(1, 8, stride=2), :]))

    lane8 = lax.broadcasted_iota(jnp.int32, (8, 128), 1)

    def pack1(kind):
        tile = jnp.zeros((8, 128), jnp.float32)
        for i in range(4):
            moved = roll(E1[4 + i, kind, 0:8, 0:128], 16 * i - 120, 1)
            tile = jnp.where((lane8 >= 16 * i) & (lane8 < 16 * i + 16), moved, tile)
        PK1[kind] = tile

    def coarsen1(get, kind):
        both = jnp.concatenate([get(0) + get(1), get(2) + get(3)], axis=0)
        pairs = pair_sum(both)
        quads = pairs + jnp.where(lane16 % 4 < 2, roll(pairs, -2, 1), roll(pairs, 2, 1))
        R1[...] = 0.25 * jnp.take_along_axis(quads, 4 * ((lane16 + 16) % 32), axis=1)
        T2[kind] = 0.25 * (R1[pl.ds(0, 8, stride=2), :] + R1[pl.ds(1, 8, stride=2), :])

    def put_c1(i, value):
        E1[4 + i, 0, 0:8, 0:128] = value

    coarsen0(lambda i: E0[3 + i, 1, 0:16, 0:128], put_c1)
    pack1(0)
    coarsen1(lambda i: E1[4 + i, 0, 0:8, 0:128], 0)

    pl.semaphore_wait(barrier, len(others))

    def side_of(oz):
        return 0 if oz == -1 else 1

    def reach0(offset, width, count, low, high):
        if offset == 0:
            return (low, count), (low, count)
        if offset == 1:
            return (low + count - width, width), (high - width, width)
        return (low, width), (low + count, width)

    lanes = pl.ds(0, 128)

    copies_a = []
    for k, (ox, oy, oz) in enumerate(NEAR):
        width = 4 - abs(ox) - abs(oy) - abs(oz)
        (ys, yc), (yd, _) = reach0(oy, width, 16, 0, 24)
        if oz == 0:
            (xs, xc), _ = reach0(ox, width, 8, 3, 3)
            xd = {0: 3, 1: 3 - width, -1: 11}[ox]
            parts = [(0, 3, xs, xc, xd, ys, yc, yd)]
            if width == 3:
                (ys2, yc2), (yd2, _) = reach0(oy, 2, 16, 0, 24)
                (xs2, xc2), _ = reach0(ox, 2, 8, 3, 3)
                xd2 = {0: 3, 1: 1, -1: 11}[ox]
                parts = [(0, 2, xs, xc, xd, ys, yc, yd), (2, 1, xs2, xc2, xd2, ys2, yc2, yd2)]
            for j, (n, count, xs, xc, xd, ys, yc, yd) in enumerate(parts):
                src = E0.at[pl.ds(xs, xc), pl.ds(n, count), pl.ds(ys, yc), lanes]
                dst = E0.at[pl.ds(xd, xc), pl.ds(n, count), pl.ds(yd, yc), lanes]
                copies_a.append(send(src, dst, a_s.at[k, j], a_r.at[k, j], (ox, oy, oz)))
        else:
            src = PK0.at[pl.ds(ys, yc)]
            dst = PZ0.at[side_of(oz), 1 - ox, pl.ds(yd, yc)]
            copies_a.append(send(src, dst, a_s.at[k, 0], a_r.at[k, 0], (ox, oy, oz)))

    def swap1(kind, send_sem, recv_sem):
        xd = {0: 4, 1: 0, -1: 8}
        ys = {0: (0, 8), 1: (4, 4), -1: (0, 4)}
        yd = {0: (0, 8), 1: (12, 4), -1: (8, 4)}
        copies = []
        for k, (ox, oy, oz) in enumerate(NEAR):
            if oz == 0:
                src = E1.at[pl.ds(4, 4), kind, pl.ds(*ys[oy]), lanes]
                dst = E1.at[pl.ds(xd[ox], 4), kind, pl.ds(*yd[oy]), lanes]
            else:
                src = PK1.at[kind, pl.ds(*ys[oy])]
                dst = PZ1.at[kind, side_of(oz), 1 - ox, pl.ds(*yd[oy])]
            copies.append(send(src, dst, send_sem.at[k], recv_sem.at[k], (ox, oy, oz)))
        return copies

    def stage_z(kind):
        return [
            send(T2.at[kind], ZR.at[kind, k], z_s.at[kind, k], z_r.at[kind, k], (0, 0, oz))
            for k, oz in enumerate(ALONG)
        ]

    def window(kind):
        ahead2, ahead1, behind1, behind2 = (ZR[kind, k] for k in range(4))
        tile = jnp.where(lane8 < 16, behind2, behind1)
        tile = jnp.where(lane8 < 48, tile, T2[kind])
        tile = jnp.where(lane8 < 80, tile, ahead1)
        tile = jnp.where(lane8 < 112, tile, ahead2)
        for i in range(2):
            S2[kind, i, 0:4] = tile[4 * i : 4 * i + 4]
            W2[kind, i, 0:4] = tile[4 * i : 4 * i + 4]

    def stage_xy(kind):
        copies = []
        for k, (ox, oy) in enumerate(PLANE):
            dx, dy = (SX - ox) % SX, (SY - oy) % SY
            src = S2.at[kind, :, pl.ds(0, 4)]
            dst = W2.at[kind, pl.ds(2 * dx, 2), pl.ds(4 * dy, 4)]
            copies.append(send(src, dst, m_s.at[kind, k], m_r.at[kind, k], (ox, oy, 0)))
        return copies

    copies_cz = stage_z(0)
    copies_c1 = swap1(0, c1_s, c1_r)

    sub8 = lax.broadcasted_iota(jnp.int32, (8, 128), 0)
    labels = []
    for x in range(SX):
        bx = lax.rem(me[0] + x, SX)
        tile = jnp.zeros((8, 128), jnp.int32)
        for y in range(SY):
            by = lax.rem(me[1] + y, SY)
            low, mid, high = (
                owner[bx, by, lax.rem(me[2] + dz + SZ, SZ)] for dz in (-1, 0, 1)
            )
            part = jnp.where(lane8 < 48, low, jnp.where(lane8 < 80, mid, high))
            tile = jnp.where(sub8 // 2 == y, part, tile)
        labels.append(tile)

    for copy in copies_a:
        copy.wait_recv()

    lane24 = lax.broadcasted_iota(jnp.int32, (24, 128), 1)
    slot = lane24 % 16
    from_below = (slot < 3) | ((slot >= 6) & (slot < 9)) | ((slot >= 12) & (slot < 14))
    for dx in range(3):
        both = jnp.where(from_below, PZ0[1, dx], PZ0[0, dx])
        for p in {0: range(0, 3), 1: range(3, 11), 2: range(11, 14)}[dx]:
            i = {0: p + 5, 1: p - 3, 2: p - 11}[dx]
            for n in range(3):
                lo, base = (16 * i + 6 * n, 125) if n < 2 else (16 * i + 12, 126)
                E0[p, n, :, 128:256] = roll(both, base - lo, 1)

    shape0 = (24, 256)
    par0 = (lax.broadcasted_iota(jnp.int32, shape0, 0) + lax.broadcasted_iota(jnp.int32, shape0, 1)) % 2

    for p in range(1, 13):
        weights, diagonal = faces(E0[p - 1, 1], E0[p, 1], E0[p + 1, 1], 1, 1.0)
        inverse = 1.0 / diagonal
        level = E0[p, 2] * inverse
        for rows, cols in quarters(beyond_block(p - 3, 8), 2, 16, 24):
            for n in range(6):
                A0[p, n, rows, cols] = (weights[n] * inverse)[rows, cols]
            A0[p, 6, rows, cols] = level[rows, cols]
        if 3 <= p < 11:
            D0[p - 3] = diagonal[0:16, 0:128]

    def point0(get, p):
        scaled = [A0[p, n] for n in range(6)]
        here = get(p)
        return relaxed(A0[p, 6], scaled, get(p - 1), here, get(p + 1), 1), here

    def colour0(get, store, planes, q, reach):
        for p in planes:
            update, here = point0(get, p)
            mixed = jnp.where(par0 == (p + 1 + q) % 2, update, here)
            for rows, cols in quarters(beyond_block(p - 3, 8), reach, 16, 24):
                store(p, rows, cols, mixed[rows, cols])

    def get_e(p):
        return E0[p, 0]

    def get_va(p):
        return VA[p - 1]

    def put_va(p, rows, cols, value):
        VA[p - 1, rows, cols] = value

    def get_vb(p):
        return VB[p - 2]

    def put_vb(p, rows, cols, value):
        VB[p - 2, rows, cols] = value

    colour0(get_e, put_va, range(1, 13), 0, 2)
    colour0(get_va, put_vb, range(2, 12), 1, 1)

    def resid0(i):
        update, here = point0(get_vb, 3 + i)
        return D0[i] * (update - here)[0:16, 0:128]

    def unpack1(kind):
        lane_16 = lax.broadcasted_iota(jnp.int32, (16, 128), 1)
        for dx in range(3):
            both = jnp.where(lane_16 % 16 < 8, PZ1[kind, 1, dx], PZ1[kind, 0, dx])
            for i in range(4):
                E1[4 * dx + i, kind, :, 128:256] = roll(both, 120 - 16 * i, 1)

    def setup1(p):
        weights, diagonal = faces(E1[p - 1, 0], E1[p, 0], E1[p + 1, 0], 2, 0.25)
        inverse = 1.0 / diagonal
        for n in range(6):
            A1[p, n] = weights[n] * inverse
        if 4 <= p < 8:
            D1[p - 4] = diagonal[0:8, 0:128]

    near1 = []
    sub256 = lax.broadcasted_iota(jnp.int32, (8, 256), 0)
    for i in range(6):
        both = pair_sum(E0[2 * i + 1, 1] + E0[2 * i + 2, 1])
        for half in range(2):
            C1[i, half] = both[:, 128 * half : 128 * half + 128]
        rows = []
        for first, count in ((0, 8), (16, 1), (22, 1)):
            if count == 8:
                halves = [C1[i, h, pl.ds(0, 8, stride=2), :] + C1[i, h, pl.ds(1, 8, stride=2), :] for h in range(2)]
                rows.append(jnp.concatenate(halves, axis=1))
            else:
                rows.append(jnp.broadcast_to(both[first : first + 1] + both[first + 1 : first + 2], (8, 256)))
        near1.append(
            0.125 * jnp.concatenate([rows[0], jnp.where(sub256 < 4, rows[1], rows[2])], axis=0)
        )
    own1 = []
    for i in range(4):
        diagonal = faces(near1[i], near1[i + 1], near1[i + 2], 2, 0.25)[1]
        own1.append(1.0 / diagonal[0:8, 0:128])

    def put_b1(i, value):
        E1[4 + i, 1, 0:8, 0:128] = value * own1[i]

    coarsen0(resid0, put_b1)
    pack1(1)
    copies_b1 = swap1(1, b1_s, b1_r)

    packed = jnp.zeros((16, 128), jnp.float32)
    for i in range(8):
        moved = roll(VB[1 + i, 0:16, 0:128], 16 * i - 126, 1)
        packed = jnp.where((lane16 >= 16 * i) & (lane16 < 16 * i + 4), moved, packed)
    PKV[...] = packed
    xs = {0: (1, 8), 1: (7, 2), -1: (1, 2)}
    xd = {0: (2, 8), 1: (0, 2), -1: (10, 2)}
    ys = {0: (0, 16), 1: (14, 2), -1: (0, 2)}
    yd = {0: (0, 16), 1: (22, 2), -1: (16, 2)}
    copies_v0 = []
    for k, (ox, oy, oz) in enumerate(CLOSE):
        if oz == 0:
            src = VB.at[pl.ds(*xs[ox]), pl.ds(*ys[oy]), lanes]
            dst = U0.at[pl.ds(*xd[ox]), pl.ds(*yd[oy]), lanes]
        else:
            src = PKV.at[pl.ds(*ys[oy])]
            dst = PZV.at[side_of(oz), 1 - ox, pl.ds(*yd[oy])]
        copies_v0.append(send(src, dst, v0_s.at[k], v0_r.at[k], (ox, oy, oz)))
    for i in range(8):
        U0[2 + i, 0:16, 0:128] = VB[1 + i, 0:16, 0:128]

    for copy in copies_c1:
        copy.wait_recv()
    unpack1(0)
    for p in range(1, 11):
        setup1(p)

    for copy in copies_cz:
        copy.wait_recv()
    window(0)
    copies_cm = stage_xy(0)

    for copy in copies_b1:
        copy.wait_recv()

    unpack1(1)
    shape1 = (16, 256)
    par1 = (
        lax.broadcasted_iota(jnp.int32, shape1, 0) + lax.broadcasted_iota(jnp.int32, shape1, 1) // 2
    ) % 2
    first1 = [jnp.where(par1 == p % 2, E1[p, 1], 0.0) for p in range(12)]

    def point1(get, p):
        scaled = [A1[p, n] for n in range(6)]
        here = get(p)
        return relaxed(E1[p, 1], scaled, get(p - 1), here, get(p + 1), 2), here

    def colour1(get, store, planes, q, reach):
        for p in planes:
            update, here = point1(get, p)
            mixed = jnp.where(par1 == (p + q) % 2, update, here)
            for rows, cols in quarters(beyond_block(p - 4, 4), reach, 8, 16):
                store(p, rows, cols, mixed[rows, cols])

    def getter(ref):
        return lambda p: ref[p]

    def putter(ref):
        def put(p, rows, cols, value):
            ref[p, rows, cols] = value
        return put

    colour1(lambda p: first1[p], putter(V1), range(1, 11), 1, 4)

    def resid1(i):
        update, here = point1(getter(V1), 4 + i)
        return D1[i] * (update - here)[0:8, 0:128]

    coarsen1(resid1, 1)
    copies_fz = stage_z(1)

    for copy in copies_cm:
        copy.wait_recv()

    def setup2(p):
        here = W2[0, p]
        weights, diagonal = faces(W2[0, (p + 15) % 16], here, W2[0, (p + 1) % 16], 1, 0.0625)
        inverse = 1.0 / diagonal
        for n in range(6):
            A2[p, n] = weights[n] * inverse
        A2[p, 6] = inverse
        D2[p] = diagonal

    def coarsen2(get, store):
        for i in range(8):
            R2[i] = pair_sum(get(2 * i) + get(2 * i + 1))
        for i in range(8):
            store(i, 0.125 * (R2[i, pl.ds(0, 8, stride=2), :] + R2[i, pl.ds(1, 8, stride=2), :]))

    def put_c3(i, value):
        E3[i] = value

    for copy in copies_fz:
        copy.wait_recv()
    window(1)
    copies_fm = stage_xy(1)

    for p in range(16):
        setup2(p)
    coarsen2(lambda i: W2[0, i], put_c3)
    z3 = ((lane8 + 16) % 32) // 2
    for x in range(8):
        weights, diagonal = faces(E3[(x + 7) % 8], E3[x], E3[(x + 1) % 8], 2, 0.015625)
        inverse = 1.0 / diagonal
        label = labels[x]
        joined = (
            label == labels[(x + 1) % 8],
            label == labels[(x + 7) % 8],
            label == roll(label, -1, 0),
            label == roll(label, 1, 0),
            z3 != 15,
            z3 != 0,
        )
        for n in range(6):
            A3[x, n] = jnp.where(joined[n], weights[n] * inverse, 0.0)
        B3[x] = inverse

    for copy in copies_fm:
        copy.wait_recv()

    shape2 = (16, 128)
    par2 = (
        lax.broadcasted_iota(jnp.int32, shape2, 0) + lax.broadcasted_iota(jnp.int32, shape2, 1)
    ) % 2
    level2 = [W2[1, p] * A2[p, 6] for p in range(16)]
    first2 = [jnp.where(par2 == p % 2, level2[p], 0.0) for p in range(16)]
    for p in range(16):
        W2[1, p] = level2[p]

    def point2(get, p):
        scaled = [A2[p, n] for n in range(6)]
        here = get(p)
        return relaxed(W2[1, p], scaled, get((p + 15) % 16), here, get((p + 1) % 16), 1), here

    def colour2(get, ref, planes, q):
        for t in planes:
            p = t % 16
            update, here = point2(get, p)
            ref[p] = jnp.where(par2 == (p + q) % 2, update, here)

    colour2(lambda p: first2[p], V2, range(16), 1)

    def resid2(p):
        update, here = point2(getter(V2), p)
        return D2[p] * (update - here)

    def put_b3(i, value):
        B3[i] = value * B3[i]

    coarsen2(resid2, put_b3)

    par3 = (sub8 + lane8 // 2 + me[0]) % 2
    def pass3(values, q):
        fresh = []
        for x in range(8):
            scaled = [A3[x, n] for n in range(6)]
            here = values[x]
            update = relaxed(B3[x], scaled, values[(x + 7) % 8], here, values[(x + 1) % 8], 2)
            fresh.append(jnp.where(par3 == (x + q) % 2, update, here))
        return tuple(fresh)

    solved = tuple(jnp.where(par3 == x % 2, B3[x], 0.0) for x in range(8))
    solved = pass3(solved, 1)
    solved = lax.fori_loop(
        0, CSWEEPS - 1, lambda t, values: pass3(pass3(values, 0), 1), solved
    )

    for x in (6, 7, 0, 1, 2):
        R2[x, pl.ds(0, 8, stride=2), :] = solved[x]
        R2[x, pl.ds(1, 8, stride=2), :] = solved[x]
    for t in range(12, 22):
        p = t % 16
        V2B[p] = V2[p] + R2[p // 2]
    colour2(getter(V2B), V2C, range(13, 21), 0)
    colour2(getter(V2C), V2B, range(14, 20), 1)

    own_lane = 48 + lane8 // 4
    halo_lane = jnp.where(lane8 < 64, 80 + lane8 // 4, 16 + lane8 // 4)
    pieces = []
    for x in range(-2, 4):
        plane = V2B[x % 16]
        pieces.append(jnp.where(sub8 < 6, plane[0:8], plane[8:16]))
    for x in range(6):
        for half, source in enumerate((own_lane, halo_lane)):
            piece = jnp.take_along_axis(pieces[x], source, axis=1)
            X1[x, half, pl.ds(0, 8, stride=2), :] = piece
            X1[x, half, pl.ds(1, 8, stride=2), :] = piece
    for p in range(1, 11):
        x = p - 4
        add = jnp.concatenate([X1[x // 2 + 2, 0], X1[x // 2 + 2, 1]], axis=1)
        V1B[p] = V1[p] + add
    colour1(getter(V1B), putter(V1C), range(2, 10), 0, 3)
    colour1(getter(V1C), putter(V1D), range(3, 9), 1, 2)

    for copy in copies_v0:
        copy.wait_recv()
    for dx in range(3):
        both = jnp.where(lane24 % 16 < 2, PZV[1, dx], PZV[0, dx])
        for p in {0: range(0, 2), 1: range(2, 10), 2: range(10, 12)}[dx]:
            i = {0: p + 6, 1: p - 2, 2: p - 10}[dx]
            U0[p, :, 128:256] = roll(both, 126 - 16 * i, 1)
    for j in range(6):
        value = V1D[3 + j]
        for half in range(2):
            piece = value[0:8, 128 * half : 128 * half + 128]
            X0[j, half, pl.ds(0, 8, stride=2), :] = piece
            X0[j, half, pl.ds(1, 8, stride=2), :] = piece
        inner = jnp.concatenate([X0[j, 0], X0[j, 1]], axis=1)
        outer = jnp.where(
            sub256 < 4,
            jnp.broadcast_to(value[8:9], (8, 256)),
            jnp.broadcast_to(value[15:16], (8, 256)),
        )
        add = jnp.concatenate([inner, outer], axis=0)
        UA[2 * j] = U0[2 * j] + add
        UA[2 * j + 1] = U0[2 * j + 1] + add

    def get_ua(p):
        return UA[p - 1]

    def get_ub(p):
        return UB[p - 2]

    def put_ub(p, rows, cols, value):
        UB[p - 2, rows, cols] = value

    def put_out(p, rows, cols, value):
        out[p - 3] = value

    colour0(get_ua, put_ub, range(2, 12), 0, 1)
    colour0(get_ub, put_out, range(3, 11), 1, 0)

    for copies in (copies_a, copies_c1, copies_cz, copies_b1, copies_v0, copies_cm, copies_fz, copies_fm):
        for copy in copies:
            copy.wait_send()


def local(source_term, conductivity, initial_guess, box_owner):
    def vmem(*shape):
        return pltpu.VMEM(shape, jnp.float32)

    dma = pltpu.SemaphoreType.DMA
    scratch = [
        vmem(14, 3, 24, 256), vmem(16, 128), vmem(2, 3, 24, 128), vmem(14, 7, 24, 256),
        vmem(8, 16, 128), vmem(12, 24, 256), vmem(10, 24, 256), vmem(12, 24, 256),
        vmem(12, 24, 256), vmem(10, 24, 256), vmem(16, 128), vmem(2, 3, 24, 128),
        vmem(4, 16, 128), vmem(6, 2, 16, 128),
        vmem(6, 2, 24, 128), vmem(12, 2, 16, 256), vmem(2, 8, 128), vmem(2, 2, 3, 16, 128), vmem(12, 6, 16, 256),
        vmem(4, 8, 128), vmem(12, 16, 256), vmem(12, 16, 256), vmem(12, 16, 256),
        vmem(12, 16, 256), vmem(6, 2, 16, 128), vmem(16, 128),
        vmem(2, 8, 128), vmem(2, 4, 8, 128), vmem(2, 2, 8, 128), vmem(2, 16, 16, 128),
        vmem(16, 16, 128), vmem(16, 16, 128), vmem(16, 16, 128), vmem(16, 7, 16, 128),
        vmem(16, 16, 128), vmem(8, 16, 128), vmem(8, 8, 128), vmem(8, 6, 8, 128),
        vmem(8, 8, 128),
        pltpu.SMEM((8, 4, 16), jnp.int32),
        dma((4,)), dma((26, 2)), dma((26, 2)), dma((26,)), dma((26,)), dma((26,)), dma((26,)),
        dma((18,)), dma((18,)), dma((2, 4)), dma((2, 4)), dma((2, 31)), dma((2, 31)),
    ]
    anywhere = pl.BlockSpec(memory_space=pltpu.HBM)
    return pl.pallas_call(
        kernel,
        out_shape=jax.ShapeDtypeStruct(source_term.shape, jnp.float32),
        in_specs=[anywhere, anywhere, anywhere, anywhere],
        out_specs=pl.BlockSpec(memory_space=pltpu.VMEM),
        scratch_shapes=scratch,
        compiler_params=pltpu.CompilerParams(
            collective_id=0, has_side_effects=True, vmem_limit_bytes=55120 << 10
        ),
    )(source_term, conductivity, initial_guess, box_owner)


def solution(mesh):
    return jax.shard_map(
        local,
        mesh=mesh,
        in_specs=(P("gx", "gy", "gz"), P("gx", "gy", "gz"), P("gx", "gy", "gz"), P()),
        out_specs=P("gx", "gy", "gz"),
        check_vma=False,
    )
```

```python
import itertools

import jax
import jax.numpy as jnp
from jax import lax
from jax.experimental import pallas as pl
from jax.experimental.pallas import tpu as pltpu
from jax.sharding import PartitionSpec as P

MESH = pl.DeviceIdType.MESH
SX, SY, SZ = 8, 4, 16
CSWEEPS = 8
screening = 0.05

NEAR = [d for d in itertools.product((-1, 0, 1), repeat=3) if d != (0, 0, 0)]
NEAR.sort(key=lambda d: (-2 * abs(d[1]) - abs(d[0]) - abs(d[2]) / 2, d))
CLOSE = [d for d in NEAR if abs(d[0]) + abs(d[1]) + abs(d[2]) <= 2]
PLANE = [d for d in itertools.product(range(SX), range(SY)) if d != (0, 0)]
PLANE.sort(key=lambda d: (-min(d[0], SX - d[0]) - 2 * min(d[1], SY - d[1]), d))
ALONG = [-2, -1, 1, 2]


def everyone():
    found = {(a % SX, b % SY, c % SZ) for a, b, c in NEAR}
    found |= {(a, b, 0) for a, b in PLANE}
    found |= {(0, 0, c % SZ) for c in ALONG}
    return sorted(found, key=lambda d: (-2 * min(d[1], SY - d[1]) - min(d[0], SX - d[0]) - min(d[2], SZ - d[2]), d))


def roll(values, shift, axis):
    shift = shift % values.shape[axis]
    return values if shift == 0 else pltpu.roll(values, shift, axis)


def around(before, here, after, step):
    return (
        after,
        before,
        roll(here, -1, 0),
        roll(here, 1, 0),
        roll(here, -step, 1),
        roll(here, step, 1),
    )


def faces(before, here, after, step, stiffness):
    half = 0.5 * stiffness
    weights = [half * (here + other) for other in around(before, here, after, step)]
    diagonal = screening + (
        (weights[0] + weights[1]) + (weights[2] + weights[3]) + (weights[4] + weights[5])
    )
    return weights, diagonal


def relaxed(level, scaled, before, here, after, step):
    sides = around(before, here, after, step)
    terms = [scaled[n] * sides[n] for n in range(6)]
    return level + (((terms[0] + terms[1]) + (terms[2] + terms[3])) + (terms[4] + terms[5]))


def beyond_block(x, count):
    return max(0, -x, x - count + 1)


def quarters(away, reach, rows, all_rows):
    inner = (slice(0, rows), slice(0, 128))
    found = [inner]
    if away + 1 <= reach:
        found += [(slice(rows, all_rows), slice(0, 128)), (slice(0, rows), slice(128, 256))]
    if away + 2 <= reach:
        found.append((slice(rows, all_rows), slice(128, 256)))
    return found


def pair_sum(values):
    lane = lax.broadcasted_iota(jnp.int32, values.shape, len(values.shape) - 1)
    return values + jnp.where(lane % 2 == 0, roll(values, -1, 1), roll(values, 1, 1))


def kernel(
    f_in, c_in, v_in, owner_in, out,
    E0, PK0, PZ0, A0, D0, VA, VB, U0, UA, UB, PKV, PZV, R0, X0,
    C1, E1, PK1, PZ1, A1, D1, V1, V1B, V1C, V1D, X1, R1,
    T2, ZR, S2, W2, V2, V2B, V2C, A2, D2, R2, E3, A3, B3, owner,
    in_sem, a_s, a_r, c1_s, c1_r, b1_s, b1_r, v0_s, v0_r, z_s, z_r, m_s, m_r,
):
    me = (lax.axis_index("gx"), lax.axis_index("gy"), lax.axis_index("gz"))

    def at(d):
        return tuple(
            lax.rem(me[i] + d[i] + size, size) for i, size in enumerate((SX, SY, SZ))
        )

    def send(src, dst, send_sem, recv_sem, d):
        copy = pltpu.make_async_remote_copy(
            src_ref=src, dst_ref=dst, send_sem=send_sem, recv_sem=recv_sem,
            device_id=at(d), device_id_type=MESH,
        )
        copy.start()
        return copy

    loads = [
        pltpu.make_async_copy(ref, E0.at[pl.ds(3, 8), n, pl.ds(0, 16), pl.ds(0, 128)], in_sem.at[n])
        for n, ref in enumerate((v_in, c_in, f_in))
    ]
    loads.append(pltpu.make_async_copy(owner_in, owner, in_sem.at[3]))
    for copy in loads:
        copy.start()
    barrier = pltpu.get_barrier_semaphore()
    others = everyone()
    for d in others:
        pl.semaphore_signal(barrier, inc=1, device_id=at(d), device_id_type=MESH)
    for copy in loads:
        copy.wait()

    lane16 = lax.broadcasted_iota(jnp.int32, (16, 128), 1)
    packed = jnp.zeros((16, 128), jnp.float32)
    for i in range(8):
        for n in range(3):
            lo, count = (16 * i + 6 * n, 6) if n < 2 else (16 * i + 12, 4)
            moved = roll(E0[3 + i, n, 0:16, 0:128], lo - (125 if n < 2 else 126), 1)
            packed = jnp.where((lane16 >= lo) & (lane16 < lo + count), moved, packed)
    PK0[...] = packed

    def coarsen0(get, store):
        for i in range(4):
            R0[i] = pair_sum(get(2 * i) + get(2 * i + 1))
        for i in range(4):
            store(i, 0.125 * (R0[i, pl.ds(0, 8, stride=2), :] + R0[i, pl.ds(1, 8, stride=2), :]))

    lane8 = lax.broadcasted_iota(jnp.int32, (8, 128), 1)

    def pack1(kind):
        tile = jnp.zeros((8, 128), jnp.float32)
        for i in range(4):
            moved = roll(E1[4 + i, kind, 0:8, 0:128], 16 * i - 120, 1)
            tile = jnp.where((lane8 >= 16 * i) & (lane8 < 16 * i + 16), moved, tile)
        PK1[kind] = tile

    def coarsen1(get, kind):
        both = jnp.concatenate([get(0) + get(1), get(2) + get(3)], axis=0)
        pairs = pair_sum(both)
        quads = pairs + jnp.where(lane16 % 4 < 2, roll(pairs, -2, 1), roll(pairs, 2, 1))
        R1[...] = 0.25 * jnp.take_along_axis(quads, 4 * ((lane16 + 16) % 32), axis=1)
        T2[kind] = 0.25 * (R1[pl.ds(0, 8, stride=2), :] + R1[pl.ds(1, 8, stride=2), :])

    def put_c1(i, value):
        E1[4 + i, 0, 0:8, 0:128] = value

    coarsen0(lambda i: E0[3 + i, 1, 0:16, 0:128], put_c1)
    pack1(0)
    coarsen1(lambda i: E1[4 + i, 0, 0:8, 0:128], 0)

    pl.semaphore_wait(barrier, len(others))

    def side_of(oz):
        return 0 if oz == -1 else 1

    def reach0(offset, width, count, low, high):
        if offset == 0:
            return (low, count), (low, count)
        if offset == 1:
            return (low + count - width, width), (high - width, width)
        return (low, width), (low + count, width)

    lanes = pl.ds(0, 128)

    copies_a = []
    for k, (ox, oy, oz) in enumerate(NEAR):
        width = 4 - abs(ox) - abs(oy) - abs(oz)
        (ys, yc), (yd, _) = reach0(oy, width, 16, 0, 24)
        if oz == 0:
            (xs, xc), _ = reach0(ox, width, 8, 3, 3)
            xd = {0: 3, 1: 3 - width, -1: 11}[ox]
            parts = [(0, 3, xs, xc, xd, ys, yc, yd)]
            if width == 3:
                (ys2, yc2), (yd2, _) = reach0(oy, 2, 16, 0, 24)
                (xs2, xc2), _ = reach0(ox, 2, 8, 3, 3)
                xd2 = {0: 3, 1: 1, -1: 11}[ox]
                parts = [(0, 2, xs, xc, xd, ys, yc, yd), (2, 1, xs2, xc2, xd2, ys2, yc2, yd2)]
            for j, (n, count, xs, xc, xd, ys, yc, yd) in enumerate(parts):
                src = E0.at[pl.ds(xs, xc), pl.ds(n, count), pl.ds(ys, yc), lanes]
                dst = E0.at[pl.ds(xd, xc), pl.ds(n, count), pl.ds(yd, yc), lanes]
                copies_a.append(send(src, dst, a_s.at[k, j], a_r.at[k, j], (ox, oy, oz)))
        else:
            src = PK0.at[pl.ds(ys, yc)]
            dst = PZ0.at[side_of(oz), 1 - ox, pl.ds(yd, yc)]
            copies_a.append(send(src, dst, a_s.at[k, 0], a_r.at[k, 0], (ox, oy, oz)))

    def swap1(kind, send_sem, recv_sem):
        xd = {0: 4, 1: 0, -1: 8}
        ys = {0: (0, 8), 1: (4, 4), -1: (0, 4)}
        yd = {0: (0, 8), 1: (12, 4), -1: (8, 4)}
        copies = []
        for k, (ox, oy, oz) in enumerate(NEAR):
            if oz == 0:
                src = E1.at[pl.ds(4, 4), kind, pl.ds(*ys[oy]), lanes]
                dst = E1.at[pl.ds(xd[ox], 4), kind, pl.ds(*yd[oy]), lanes]
            else:
                src = PK1.at[kind, pl.ds(*ys[oy])]
                dst = PZ1.at[kind, side_of(oz), 1 - ox, pl.ds(*yd[oy])]
            copies.append(send(src, dst, send_sem.at[k], recv_sem.at[k], (ox, oy, oz)))
        return copies

    def stage_z(kind):
        return [
            send(T2.at[kind], ZR.at[kind, k], z_s.at[kind, k], z_r.at[kind, k], (0, 0, oz))
            for k, oz in enumerate(ALONG)
        ]

    def window(kind):
        ahead2, ahead1, behind1, behind2 = (ZR[kind, k] for k in range(4))
        tile = jnp.where(lane8 < 16, behind2, behind1)
        tile = jnp.where(lane8 < 48, tile, T2[kind])
        tile = jnp.where(lane8 < 80, tile, ahead1)
        tile = jnp.where(lane8 < 112, tile, ahead2)
        for i in range(2):
            S2[kind, i, 0:4] = tile[4 * i : 4 * i + 4]
            W2[kind, i, 0:4] = tile[4 * i : 4 * i + 4]

    def stage_xy(kind):
        copies = []
        for k, (ox, oy) in enumerate(PLANE):
            dx, dy = (SX - ox) % SX, (SY - oy) % SY
            src = S2.at[kind, :, pl.ds(0, 4)]
            dst = W2.at[kind, pl.ds(2 * dx, 2), pl.ds(4 * dy, 4)]
            copies.append(send(src, dst, m_s.at[kind, k], m_r.at[kind, k], (ox, oy, 0)))
        return copies

    copies_cz = stage_z(0)
    copies_c1 = swap1(0, c1_s, c1_r)

    sub8 = lax.broadcasted_iota(jnp.int32, (8, 128), 0)
    labels = []
    for x in range(SX):
        bx = lax.rem(me[0] + x, SX)
        tile = jnp.zeros((8, 128), jnp.int32)
        for y in range(SY):
            by = lax.rem(me[1] + y, SY)
            low, mid, high = (
                owner[bx, by, lax.rem(me[2] + dz + SZ, SZ)] for dz in (-1, 0, 1)
            )
            part = jnp.where(lane8 < 48, low, jnp.where(lane8 < 80, mid, high))
            tile = jnp.where(sub8 // 2 == y, part, tile)
        labels.append(tile)

    for copy in copies_a:
        copy.wait_recv()

    lane24 = lax.broadcasted_iota(jnp.int32, (24, 128), 1)
    slot = lane24 % 16
    from_below = (slot < 3) | ((slot >= 6) & (slot < 9)) | ((slot >= 12) & (slot < 14))
    for dx in range(3):
        both = jnp.where(from_below, PZ0[1, dx], PZ0[0, dx])
        for p in {0: range(0, 3), 1: range(3, 11), 2: range(11, 14)}[dx]:
            i = {0: p + 5, 1: p - 3, 2: p - 11}[dx]
            for n in range(3):
                lo, base = (16 * i + 6 * n, 125) if n < 2 else (16 * i + 12, 126)
                E0[p, n, :, 128:256] = roll(both, base - lo, 1)

    shape0 = (24, 256)
    par0 = (lax.broadcasted_iota(jnp.int32, shape0, 0) + lax.broadcasted_iota(jnp.int32, shape0, 1)) % 2

    for p in range(1, 13):
        weights, diagonal = faces(E0[p - 1, 1], E0[p, 1], E0[p + 1, 1], 1, 1.0)
        inverse = 1.0 / diagonal
        level = E0[p, 2] * inverse
        for rows, cols in quarters(beyond_block(p - 3, 8), 2, 16, 24):
            for n in range(6):
                A0[p, n, rows, cols] = (weights[n] * inverse)[rows, cols]
            A0[p, 6, rows, cols] = level[rows, cols]
        if 3 <= p < 11:
            D0[p - 3] = diagonal[0:16, 0:128]

    def point0(get, p):
        scaled = [A0[p, n] for n in range(6)]
        here = get(p)
        return relaxed(A0[p, 6], scaled, get(p - 1), here, get(p + 1), 1), here

    def colour0(get, store, planes, q, reach):
        for p in planes:
            update, here = point0(get, p)
            mixed = jnp.where(par0 == (p + 1 + q) % 2, update, here)
            for rows, cols in quarters(beyond_block(p - 3, 8), reach, 16, 24):
                store(p, rows, cols, mixed[rows, cols])

    def get_e(p):
        return E0[p, 0]

    def get_va(p):
        return VA[p - 1]

    def put_va(p, rows, cols, value):
        VA[p - 1, rows, cols] = value

    def get_vb(p):
        return VB[p - 2]

    def put_vb(p, rows, cols, value):
        VB[p - 2, rows, cols] = value

    colour0(get_e, put_va, range(1, 13), 0, 2)
    colour0(get_va, put_vb, range(2, 12), 1, 1)

    def resid0(i):
        update, here = point0(get_vb, 3 + i)
        return D0[i] * (update - here)[0:16, 0:128]

    def unpack1(kind):
        lane_16 = lax.broadcasted_iota(jnp.int32, (16, 128), 1)
        for dx in range(3):
            both = jnp.where(lane_16 % 16 < 8, PZ1[kind, 1, dx], PZ1[kind, 0, dx])
            for i in range(4):
                E1[4 * dx + i, kind, :, 128:256] = roll(both, 120 - 16 * i, 1)

    def setup1(p):
        weights, diagonal = faces(E1[p - 1, 0], E1[p, 0], E1[p + 1, 0], 2, 0.25)
        inverse = 1.0 / diagonal
        for n in range(6):
            A1[p, n] = weights[n] * inverse
        if 4 <= p < 8:
            D1[p - 4] = diagonal[0:8, 0:128]

    near1 = []
    sub256 = lax.broadcasted_iota(jnp.int32, (8, 256), 0)
    for i in range(6):
        both = pair_sum(E0[2 * i + 1, 1] + E0[2 * i + 2, 1])
        for half in range(2):
            C1[i, half] = both[:, 128 * half : 128 * half + 128]
        rows = []
        for first, count in ((0, 8), (16, 1), (22, 1)):
            if count == 8:
                halves = [C1[i, h, pl.ds(0, 8, stride=2), :] + C1[i, h, pl.ds(1, 8, stride=2), :] for h in range(2)]
                rows.append(jnp.concatenate(halves, axis=1))
            else:
                rows.append(jnp.broadcast_to(both[first : first + 1] + both[first + 1 : first + 2], (8, 256)))
        near1.append(
            0.125 * jnp.concatenate([rows[0], jnp.where(sub256 < 4, rows[1], rows[2])], axis=0)
        )
    own1 = []
    for i in range(4):
        diagonal = faces(near1[i], near1[i + 1], near1[i + 2], 2, 0.25)[1]
        own1.append(1.0 / diagonal[0:8, 0:128])

    def put_b1(i, value):
        E1[4 + i, 1, 0:8, 0:128] = value * own1[i]

    coarsen0(resid0, put_b1)
    pack1(1)
    copies_b1 = swap1(1, b1_s, b1_r)

    packed = jnp.zeros((16, 128), jnp.float32)
    for i in range(8):
        moved = roll(VB[1 + i, 0:16, 0:128], 16 * i - 126, 1)
        packed = jnp.where((lane16 >= 16 * i) & (lane16 < 16 * i + 4), moved, packed)
    PKV[...] = packed
    xs = {0: (1, 8), 1: (7, 2), -1: (1, 2)}
    xd = {0: (2, 8), 1: (0, 2), -1: (10, 2)}
    ys = {0: (0, 16), 1: (14, 2), -1: (0, 2)}
    yd = {0: (0, 16), 1: (22, 2), -1: (16, 2)}
    copies_v0 = []
    for k, (ox, oy, oz) in enumerate(CLOSE):
        if oz == 0:
            src = VB.at[pl.ds(*xs[ox]), pl.ds(*ys[oy]), lanes]
            dst = U0.at[pl.ds(*xd[ox]), pl.ds(*yd[oy]), lanes]
        else:
            src = PKV.at[pl.ds(*ys[oy])]
            dst = PZV.at[side_of(oz), 1 - ox, pl.ds(*yd[oy])]
        copies_v0.append(send(src, dst, v0_s.at[k], v0_r.at[k], (ox, oy, oz)))
    for i in range(8):
        U0[2 + i, 0:16, 0:128] = VB[1 + i, 0:16, 0:128]

    for copy in copies_c1:
        copy.wait_recv()
    unpack1(0)
    for p in range(1, 11):
        setup1(p)

    for copy in copies_cz:
        copy.wait_recv()
    window(0)
    copies_cm = stage_xy(0)

    for copy in copies_b1:
        copy.wait_recv()

    unpack1(1)
    shape1 = (16, 256)
    par1 = (
        lax.broadcasted_iota(jnp.int32, shape1, 0) + lax.broadcasted_iota(jnp.int32, shape1, 1) // 2
    ) % 2
    first1 = [jnp.where(par1 == p % 2, E1[p, 1], 0.0) for p in range(12)]

    def point1(get, p):
        scaled = [A1[p, n] for n in range(6)]
        here = get(p)
        return relaxed(E1[p, 1], scaled, get(p - 1), here, get(p + 1), 2), here

    def colour1(get, store, planes, q, reach):
        for p in planes:
            update, here = point1(get, p)
            mixed = jnp.where(par1 == (p + q) % 2, update, here)
            for rows, cols in quarters(beyond_block(p - 4, 4), reach, 8, 16):
                store(p, rows, cols, mixed[rows, cols])

    def getter(ref):
        return lambda p: ref[p]

    def putter(ref):
        def put(p, rows, cols, value):
            ref[p, rows, cols] = value
        return put

    colour1(lambda p: first1[p], putter(V1), range(1, 11), 1, 4)

    def resid1(i):
        update, here = point1(getter(V1), 4 + i)
        return D1[i] * (update - here)[0:8, 0:128]

    coarsen1(resid1, 1)
    copies_fz = stage_z(1)

    for copy in copies_cm:
        copy.wait_recv()

    def setup2(p):
        here = W2[0, p]
        weights, diagonal = faces(W2[0, (p + 15) % 16], here, W2[0, (p + 1) % 16], 1, 0.0625)
        inverse = 1.0 / diagonal
        for n in range(6):
            A2[p, n] = weights[n] * inverse
        A2[p, 6] = inverse
        D2[p] = diagonal

    def coarsen2(get, store):
        for i in range(8):
            R2[i] = pair_sum(get(2 * i) + get(2 * i + 1))
        for i in range(8):
            store(i, 0.125 * (R2[i, pl.ds(0, 8, stride=2), :] + R2[i, pl.ds(1, 8, stride=2), :]))

    def put_c3(i, value):
        E3[i] = value

    for copy in copies_fz:
        copy.wait_recv()
    window(1)
    copies_fm = stage_xy(1)

    for p in range(16):
        setup2(p)
    coarsen2(lambda i: W2[0, i], put_c3)
    z3 = ((lane8 + 16) % 32) // 2
    for x in range(8):
        weights, diagonal = faces(E3[(x + 7) % 8], E3[x], E3[(x + 1) % 8], 2, 0.015625)
        inverse = 1.0 / diagonal
        label = labels[x]
        joined = (
            label == labels[(x + 1) % 8],
            label == labels[(x + 7) % 8],
            label == roll(label, -1, 0),
            label == roll(label, 1, 0),
            z3 != 15,
            z3 != 0,
        )
        for n in range(6):
            A3[x, n] = jnp.where(joined[n], weights[n] * inverse, 0.0)
        B3[x] = inverse

    for copy in copies_fm:
        copy.wait_recv()

    shape2 = (16, 128)
    par2 = (
        lax.broadcasted_iota(jnp.int32, shape2, 0) + lax.broadcasted_iota(jnp.int32, shape2, 1)
    ) % 2
    level2 = [W2[1, p] * A2[p, 6] for p in range(16)]
    first2 = [jnp.where(par2 == p % 2, level2[p], 0.0) for p in range(16)]
    for p in range(16):
        W2[1, p] = level2[p]

    def point2(get, p):
        scaled = [A2[p, n] for n in range(6)]
        here = get(p)
        return relaxed(W2[1, p], scaled, get((p + 15) % 16), here, get((p + 1) % 16), 1), here

    def colour2(get, ref, planes, q):
        for t in planes:
            p = t % 16
            update, here = point2(get, p)
            ref[p] = jnp.where(par2 == (p + q) % 2, update, here)

    colour2(lambda p: first2[p], V2, range(16), 1)

    def resid2(p):
        update, here = point2(getter(V2), p)
        return D2[p] * (update - here)

    def put_b3(i, value):
        B3[i] = value * B3[i]

    coarsen2(resid2, put_b3)

    par3 = (sub8 + lane8 // 2 + me[0]) % 2
    def pass3(values, q):
        fresh = []
        for x in range(8):
            scaled = [A3[x, n] for n in range(6)]
            here = values[x]
            update = relaxed(B3[x], scaled, values[(x + 7) % 8], here, values[(x + 1) % 8], 2)
            fresh.append(jnp.where(par3 == (x + q) % 2, update, here))
        return tuple(fresh)

    solved = tuple(jnp.where(par3 == x % 2, B3[x], 0.0) for x in range(8))
    solved = pass3(solved, 1)
    solved = lax.fori_loop(
        0, CSWEEPS - 1, lambda t, values: pass3(pass3(values, 0), 1), solved
    )

    for x in (6, 7, 0, 1, 2):
        R2[x, pl.ds(0, 8, stride=2), :] = solved[x]
        R2[x, pl.ds(1, 8, stride=2), :] = solved[x]
    for t in range(12, 22):
        p = t % 16
        V2B[p] = V2[p] + R2[p // 2]
    colour2(getter(V2B), V2C, range(13, 21), 0)
    colour2(getter(V2C), V2B, range(14, 20), 1)

    own_lane = 48 + lane8 // 4
    halo_lane = jnp.where(lane8 < 64, 80 + lane8 // 4, 16 + lane8 // 4)
    pieces = []
    for x in range(-2, 4):
        plane = V2B[x % 16]
        pieces.append(jnp.where(sub8 < 6, plane[0:8], plane[8:16]))
    for x in range(6):
        for half, source in enumerate((own_lane, halo_lane)):
            piece = jnp.take_along_axis(pieces[x], source, axis=1)
            X1[x, half, pl.ds(0, 8, stride=2), :] = piece
            X1[x, half, pl.ds(1, 8, stride=2), :] = piece
    for p in range(1, 11):
        x = p - 4
        add = jnp.concatenate([X1[x // 2 + 2, 0], X1[x // 2 + 2, 1]], axis=1)
        V1B[p] = V1[p] + add
    colour1(getter(V1B), putter(V1C), range(2, 10), 0, 3)
    colour1(getter(V1C), putter(V1D), range(3, 9), 1, 2)

    for copy in copies_v0:
        copy.wait_recv()
    for dx in range(3):
        both = jnp.where(lane24 % 16 < 2, PZV[1, dx], PZV[0, dx])
        for p in {0: range(0, 2), 1: range(2, 10), 2: range(10, 12)}[dx]:
            i = {0: p + 6, 1: p - 2, 2: p - 10}[dx]
            U0[p, :, 128:256] = roll(both, 126 - 16 * i, 1)
    for j in range(6):
        value = V1D[3 + j]
        for half in range(2):
            piece = value[0:8, 128 * half : 128 * half + 128]
            X0[j, half, pl.ds(0, 8, stride=2), :] = piece
            X0[j, half, pl.ds(1, 8, stride=2), :] = piece
        inner = jnp.concatenate([X0[j, 0], X0[j, 1]], axis=1)
        outer = jnp.where(
            sub256 < 4,
            jnp.broadcast_to(value[8:9], (8, 256)),
            jnp.broadcast_to(value[15:16], (8, 256)),
        )
        add = jnp.concatenate([inner, outer], axis=0)
        UA[2 * j] = U0[2 * j] + add
        UA[2 * j + 1] = U0[2 * j + 1] + add

    def get_ua(p):
        return UA[p - 1]

    def get_ub(p):
        return UB[p - 2]

    def put_ub(p, rows, cols, value):
        UB[p - 2, rows, cols] = value

    def put_out(p, rows, cols, value):
        out[p - 3] = value

    colour0(get_ua, put_ub, range(2, 12), 0, 1)
    colour0(get_ub, put_out, range(3, 11), 1, 0)

    for copies in (copies_a, copies_c1, copies_cz, copies_b1, copies_v0, copies_cm, copies_fz, copies_fm):
        for copy in copies:
            copy.wait_send()


def local(source_term, conductivity, initial_guess, box_owner):
    def vmem(*shape):
        return pltpu.VMEM(shape, jnp.float32)

    dma = pltpu.SemaphoreType.DMA
    scratch = [
        vmem(14, 3, 24, 256), vmem(16, 128), vmem(2, 3, 24, 128), vmem(14, 7, 24, 256),
        vmem(8, 16, 128), vmem(12, 24, 256), vmem(10, 24, 256), vmem(12, 24, 256),
        vmem(12, 24, 256), vmem(10, 24, 256), vmem(16, 128), vmem(2, 3, 24, 128),
        vmem(4, 16, 128), vmem(6, 2, 16, 128),
        vmem(6, 2, 24, 128), vmem(12, 2, 16, 256), vmem(2, 8, 128), vmem(2, 2, 3, 16, 128), vmem(12, 6, 16, 256),
        vmem(4, 8, 128), vmem(12, 16, 256), vmem(12, 16, 256), vmem(12, 16, 256),
        vmem(12, 16, 256), vmem(6, 2, 16, 128), vmem(16, 128),
        vmem(2, 8, 128), vmem(2, 4, 8, 128), vmem(2, 2, 8, 128), vmem(2, 16, 16, 128),
        vmem(16, 16, 128), vmem(16, 16, 128), vmem(16, 16, 128), vmem(16, 7, 16, 128),
        vmem(16, 16, 128), vmem(8, 16, 128), vmem(8, 8, 128), vmem(8, 6, 8, 128),
        vmem(8, 8, 128),
        pltpu.SMEM((8, 4, 16), jnp.int32),
        dma((4,)), dma((26, 2)), dma((26, 2)), dma((26,)), dma((26,)), dma((26,)), dma((26,)),
        dma((18,)), dma((18,)), dma((2, 4)), dma((2, 4)), dma((2, 31)), dma((2, 31)),
    ]
    anywhere = pl.BlockSpec(memory_space=pltpu.HBM)
    return pl.pallas_call(
        kernel,
        out_shape=jax.ShapeDtypeStruct(source_term.shape, jnp.float32),
        in_specs=[anywhere, anywhere, anywhere, anywhere],
        out_specs=pl.BlockSpec(memory_space=pltpu.VMEM),
        scratch_shapes=scratch,
        compiler_params=pltpu.CompilerParams(
            collective_id=0, has_side_effects=True, vmem_limit_bytes=55120 << 10
        ),
    )(source_term, conductivity, initial_guess, box_owner)


def solution(mesh):
    return jax.shard_map(
        local,
        mesh=mesh,
        in_specs=(P("gx", "gy", "gz"), P("gx", "gy", "gz"), P("gx", "gy", "gz"), P()),
        out_specs=P("gx", "gy", "gz"),
        check_vma=False,
    )
```
